32 devices in a mesh: ao: 4 (over z), gen: 4 (over y, core), act: 2 (over x).
Axes of the slice: x: 2, y: 2, z: 4, core: 2. Of those that a mesh axis runs over, the one named last changes fastest.
Arguments:
- integrals: bfloat16 [384, 2, 128, 1152], P(('ao', 'gen', 'act')), may hold values from -6 to 6
- bra_rows: bfloat16 [384, 2, 128, 16], P(('ao', 'gen', 'act')), may hold values from -0.02734375 to 0.02734375
- ket_rows: bfloat16 [384, 2, 128, 48], P(('ao', 'gen', 'act')), may hold values from -6 to 6
- block_count: int32 [32], P(('ao', 'gen', 'act')), may hold values from 1 to 12, as said below
- pair_count: int32 [384], P(('ao', 'gen', 'act')), may hold values from 32 to 128
Outputs:
- transformed: float32 [2, 16, 48, 1152], P(None, 'gen', 'act', 'ao')
The draws below stay inside these ranges and needn't reach their ends.
Inputs may be any that keep to these rules, and one draw needn't show every extreme that they name: `block_count`: one device holds exactly 12 live blocks. Rows from pair_count on are padding.
All inputs are finite; a program needn't handle non-finite values.
Results may differ from the reference program's by a relative error of at most 0.0042.
Values may be sent and summed in bfloat16 or wider, within the bound.
No kernel may reach another device: no remote copies, remote signals or barrier semaphores. Data moves between devices by JAX's collectives and lax.ppermute only.
A program may use at most 128 MiB of HBM per device.

```python
import jax
import jax.numpy as jnp
from jax import lax

NBLK = 12
BLOCK = 128
P_SIZE = 16
U = 48
VW = 1152
NB_ALL = 384
DEVICES = 32


def draw_block_count(key, part):
    keyed = jax.random.fold_in(key, 7)
    counts = jax.random.randint(keyed, (DEVICES,), 1, max(2, 2 * NBLK // 3))
    chosen = jax.random.randint(jax.random.fold_in(keyed, 1), (), 0, DEVICES)
    return jnp.where(jnp.arange(DEVICES) == chosen, NBLK, counts).astype(jnp.int32)


def place_ends(result, own_key, low, largest):
    index_at = [jax.random.randint(jax.random.fold_in(own_key, axis), (), 0, length) for axis, length in enumerate(result.shape)]
    widest = result.shape.index(max(result.shape))
    neighbour = index_at[:widest] + [(index_at[widest] + 1) % result.shape[widest]] + index_at[widest + 1:]
    return result.at[tuple(index_at)].set(low).at[tuple(neighbour)].set(largest)


def raised(result, rng, source, target, shards_of, factor):
    owner, partner = [(jnp.arange(result.shape[position]) // (result.shape[position] // shards_of)).reshape([-1 if axis == position else 1 for axis in range(result.ndim)]) for position in (source, target)]
    chosen = jax.random.permutation(rng, shards_of)[partner]
    strong = (owner == chosen) | (owner == (partner + shards_of // 2) % shards_of)
    return jnp.where(strong, factor * result, result)


def level_of(rng, extent, cuts, smallest, high):
    gain = 1.0
    for position, blocks in cuts:
        heights = jax.random.uniform(jax.random.fold_in(jax.random.fold_in(rng, 6), position), (blocks,), jnp.float32, smallest / len(cuts), high / len(cuts))
        gain = gain * jnp.repeat(jnp.exp(heights), extent[position] // blocks).reshape((-1,) + (1,) * (len(extent) - 1 - position))
    return gain


def bell_draw(stream_key, shape, spread, limit, shards=(), kind=jnp.bfloat16):
    loudness = level_of(stream_key, shape, shards, -0.22, 0.18) if shards else 1.0
    result = jax.random.normal(stream_key, shape, jnp.float32) * spread * loudness
    return jnp.minimum(jnp.maximum(result, -limit), limit).astype(kind)


def gaussian_with(own_key, dims, deviation, most, cuts, heavy, kind=jnp.bfloat16):
    drawn = deviation * jax.random.normal(own_key, dims, jnp.float32)
    if cuts:
        drawn = drawn * level_of(own_key, dims, cuts, -0.22, 0.18)
    return jnp.clip(raised(drawn, jax.random.fold_in(own_key, 3), *heavy), -most, most).astype(kind)


def setup_inputs(seed: int = 0) -> dict:
    streams_of = jax.random.split(jax.random.key(seed), 6)
    return {
        "integrals": gaussian_with(streams_of[0], (NB_ALL, 2, BLOCK, VW), 1.0, 6.0, ((0, 32),), (0, 3, 32, 2.75)),
        "bra_rows": bell_draw(streams_of[1], (NB_ALL, 2, BLOCK, P_SIZE), (DEVICES * NBLK * BLOCK) ** -0.5, 0.02734375, ((0, 32),)),
        "ket_rows": bell_draw(streams_of[2], (NB_ALL, 2, BLOCK, U), 1.0, 6.0, ((0, 32),)),
        "block_count": draw_block_count(jax.random.fold_in(streams_of[5], 71), 0),
        "pair_count": place_ends(jax.random.randint(streams_of[4], (NB_ALL,), BLOCK // 4, BLOCK + 1), jax.random.fold_in(streams_of[4], 1), BLOCK // 4, BLOCK).astype(jnp.int32),
    }


def block_product(ints_block, bra_block, ket_block):
    bra_wide = bra_block.astype(jnp.float32)
    ket_wide = ket_block.astype(jnp.float32)
    real_part = bra_wide[0][:, :, None] * ket_wide[0][:, None, :] + bra_wide[1][:, :, None] * ket_wide[1][:, None, :]
    imag_part = bra_wide[0][:, :, None] * ket_wide[1][:, None, :] - bra_wide[1][:, :, None] * ket_wide[0][:, None, :]
    rows = bra_block.shape[1]
    real_low = real_part.reshape(rows, -1).T.astype(jnp.bfloat16)
    imag_low = imag_part.reshape(rows, -1).T.astype(jnp.bfloat16)
    upper = jnp.concatenate([real_low, -imag_low], axis=1)
    lower = jnp.concatenate([imag_low, real_low], axis=1)
    weights = jnp.concatenate([upper, lower], axis=0)
    stacked = ints_block.reshape(2 * rows, -1)
    return jnp.dot(weights, stacked, preferred_element_type=jnp.float32)


def reference(integrals, bra_rows, ket_rows, block_count, pair_count):
    slots_all = integrals.shape[0]
    per_device = slots_all // block_count.shape[0]
    positions = jnp.arange(slots_all, dtype=jnp.int32)
    owners = positions // per_device
    alive = (positions % per_device) < block_count[owners]
    pair_mask = (jnp.arange(BLOCK, dtype=jnp.int32)[None, :] < pair_count[:, None]).astype(jnp.bfloat16)
    order = jnp.argsort(1 - alive.astype(jnp.int32), stable=True).astype(jnp.int32)
    live_total = jnp.sum(alive.astype(jnp.int32))
    init = jnp.zeros((2 * P_SIZE * U, VW), jnp.float32)

    def accumulate(step_number, totals):
        chosen = order[step_number]
        ints_block = lax.dynamic_index_in_dim(integrals, chosen, 0, keepdims=False)
        bra_block = lax.dynamic_index_in_dim(bra_rows, chosen, 0, keepdims=False)
        ket_block = lax.dynamic_index_in_dim(ket_rows, chosen, 0, keepdims=False)
        mask_row = lax.dynamic_index_in_dim(pair_mask, chosen, 0, keepdims=False)
        ket_block = ket_block * mask_row[None, :, None]
        return totals + block_product(ints_block, bra_block, ket_block)

    totals = lax.fori_loop(0, live_total, accumulate, init)
    return totals.reshape(2, P_SIZE, U, VW)
```

```python
import functools

import jax
import jax.numpy as jnp
from jax import lax
from jax.experimental import pallas as pl
from jax.experimental.pallas import tpu as pltpu
from jax.sharding import PartitionSpec as P

LANES = 128
GRAIN = 16
CHUNKS = 2


def relative_order(size):
    return [r for r in range(size) if r % 2 == 0] + [r for r in range(size) if r % 2 == 1]


def product_kernel(
    dims, chunk, count_ref, pairs_ref, where_ref, bra_ref, ket_ref, ints_ref,
    keep_ref, send_ref, packed, bra_pack, ket_pack, weights, spare, offsets, sems,
):
    blocks, width, general, active, gen_size, act_size = dims
    p_own = general // gen_size
    p_chunk = p_own // CHUNKS
    u_own = active // act_size
    live = count_ref[0]
    pieces = []
    size = width
    while size >= GRAIN:
        pieces.append(size)
        size //= 2

    def rows_of(b):
        return (pairs_ref[b] + GRAIN - 1) // GRAIN * GRAIN

    def place(b, total):
        offsets[b] = total
        return total + rows_of(b)

    total = lax.fori_loop(0, live, place, 0)
    tiles = (total + LANES - 1) // LANES

    def clear(i, _):
        row = pl.multiple_of(total + i * GRAIN, GRAIN)
        packed[:, pl.ds(row, GRAIN), :] = jnp.zeros((2, GRAIN, packed.shape[2]), packed.dtype)
        return 0

    lax.fori_loop(0, (tiles * LANES - total) // GRAIN, clear, 0)

    def copies(b, act):
        rows = rows_of(b)
        start = pl.multiple_of(offsets[b], GRAIN)
        for piece in pieces:
            @pl.when((rows & piece) != 0)
            def _():
                first = pl.multiple_of(rows & ~(2 * piece - 1), GRAIN)
                copy = pltpu.make_async_copy(
                    ints_ref.at[b, :, pl.ds(first, piece), :],
                    packed.at[:, pl.ds(start + first, piece), :],
                    sems.at[b],
                )
                act(copy)

    @pl.loop(0, live)
    def _(b):
        copies(b, lambda c: c.start())

    @pl.loop(0, tiles + 1)
    def _(t):
        bra_pack[t] = jnp.zeros(bra_pack.shape[1:], jnp.float32)
        ket_pack[t] = jnp.zeros(ket_pack.shape[1:], jnp.float32)

    @pl.loop(0, live)
    def _(b):
        start = offsets[b]
        tile = start // LANES
        turn = start % LANES
        lane = lax.broadcasted_iota(jnp.int32, (1, LANES), 1)
        for source, target in ((bra_ref, bra_pack), (ket_ref, ket_pack)):
            value = source[b].reshape(target.shape[1:]).astype(jnp.float32)
            value = jnp.where(lane < pairs_ref[b], value, 0.0)
            value = pltpu.roll(value, turn, 1)
            target[tile] += jnp.where(lane >= turn, value, 0.0)
            target[tile + 1] += jnp.where(lane < turn, value, 0.0)

    keep_ref[...] = jnp.zeros_like(keep_ref)
    spare[...] = jnp.zeros_like(spare)
    me_gen = where_ref[0]
    me_act = where_ref[1]
    half = keep_ref.shape[0]
    span = p_chunk * u_own

    def step(t, ready):
        def pending(b):
            return jnp.logical_and(b < live, offsets[jnp.minimum(b, blocks - 1)] < (t + 1) * LANES)

        def arrive(b):
            copies(b, lambda c: c.wait())
            return b + 1

        ready = lax.while_loop(pending, arrive, ready)
        row = 0
        for g in relative_order(gen_size):
            p_first = (me_gen ^ g) * p_own + chunk * p_chunk
            for a in range(act_size):
                u_first = pl.multiple_of((me_act ^ a) * u_own, 8)
                ket_re = ket_pack[t, pl.ds(u_first, u_own), :]
                ket_im = ket_pack[t, pl.ds(active + u_first, u_own), :]
                real, imag = [], []
                for p in range(p_chunk):
                    bra_re = bra_pack[t, pl.ds(p_first + p, 1), :]
                    bra_im = bra_pack[t, pl.ds(general + p_first + p, 1), :]
                    real.append(bra_re * ket_re + bra_im * ket_im)
                    imag.append(bra_re * ket_im - bra_im * ket_re)
                real = jnp.concatenate(real, axis=0)
                imag = jnp.concatenate(imag, axis=0)
                real_low = real.astype(jnp.bfloat16)
                imag_low = imag.astype(jnp.bfloat16)
                weights[row : row + span, :LANES] = real_low
                weights[row : row + span, LANES:] = (-imag).astype(jnp.bfloat16)
                weights[row + span : row + 2 * span, :LANES] = imag_low
                weights[row + span : row + 2 * span, LANES:] = real_low
                row += 2 * span
        first = pl.multiple_of(t * LANES, LANES)
        values = jnp.concatenate(
            [packed[0, pl.ds(first, LANES), :], packed[1, pl.ds(first, LANES), :]], axis=0
        )
        keep_ref[...] += jnp.dot(weights[:half], values, preferred_element_type=jnp.float32)
        spare[...] += jnp.dot(weights[half:], values, preferred_element_type=jnp.float32)
        return ready

    lax.fori_loop(0, tiles, step, 0)
    send_ref[...] = spare[...].astype(send_ref.dtype)


def products(chunk, sizes, count, pairs, where, bra, ket, integrals):
    blocks, _, width, columns = integrals.shape
    general, active = bra.shape[2], ket.shape[2]
    gen_size, act_size = sizes
    rows = 2 * general * active // CHUNKS
    dims = (blocks, width, general, active, gen_size, act_size)
    tiles = blocks * width // LANES
    flops = 2 * rows * 2 * blocks * width * columns // 2
    smem = pl.BlockSpec(memory_space=pltpu.SMEM)
    vmem = pl.BlockSpec(memory_space=pltpu.VMEM)
    return pl.pallas_call(
        functools.partial(product_kernel, dims, chunk),
        out_shape=(
            jax.ShapeDtypeStruct((rows // 2, columns), jnp.float32),
            jax.ShapeDtypeStruct((rows // 2, columns), jnp.bfloat16),
        ),
        in_specs=[smem, smem, smem, vmem, vmem, pl.BlockSpec(memory_space=pl.ANY)],
        out_specs=(vmem, vmem),
        scratch_shapes=[
            pltpu.VMEM((2, blocks * width, columns), jnp.bfloat16),
            pltpu.VMEM((tiles + 1, 2 * general, LANES), jnp.float32),
            pltpu.VMEM((tiles + 1, 2 * active, LANES), jnp.float32),
            pltpu.VMEM((rows, 2 * LANES), jnp.bfloat16),
            pltpu.VMEM((rows // 2, columns), jnp.float32),
            pltpu.SMEM((blocks,), jnp.int32),
            pltpu.SemaphoreType.DMA((blocks,)),
        ],
        compiler_params=pltpu.CompilerParams(vmem_limit_bytes=40 * 2**20),
        cost_estimate=pl.CostEstimate(
            flops=flops, bytes_accessed=integrals.size * 2 + rows * columns * 3, transcendentals=0
        ),
        name=f"products_{chunk}",
    )(count, pairs, where, bra, ket, integrals)


def window_of(columns, parts):
    own = columns // parts
    starts = [own * a // LANES * LANES for a in range(parts)]
    ends = [-(-own * (a + 1) // LANES) * LANES for a in range(parts)]
    return own, max(e - s for s, e in zip(starts, ends))


def plane_sum_kernel(parts, columns, where_ref, own_ref, *refs):
    own, width = window_of(columns, parts)
    received, outs, total = refs[: -parts - 1], refs[-parts - 1 : -1], refs[-1]
    value = own_ref[...]
    for ref in received:
        value = value + ref[...].astype(jnp.float32)
    total[...] = value
    me = where_ref[2]
    for k in range(parts):
        first = jnp.minimum((me ^ k) * own // LANES * LANES, columns - width)
        cut = total[:, pl.ds(pl.multiple_of(first, LANES), width)]
        outs[k][...] = cut.astype(outs[k].dtype)


def plane_sum(parts, where, own, received):
    rows, columns = own.shape
    _, width = window_of(columns, parts)
    vmem = pl.BlockSpec(memory_space=pltpu.VMEM)
    return pl.pallas_call(
        functools.partial(plane_sum_kernel, parts, columns),
        out_shape=tuple(
            jax.ShapeDtypeStruct((rows, width), jnp.float32 if k == 0 else jnp.bfloat16)
            for k in range(parts)
        ),
        in_specs=[pl.BlockSpec(memory_space=pltpu.SMEM)] + [vmem] * (1 + len(received)),
        out_specs=tuple([vmem] * parts),
        scratch_shapes=[pltpu.VMEM((rows, columns), jnp.float32)],
        cost_estimate=pl.CostEstimate(
            flops=rows * columns * 4, bytes_accessed=rows * columns * 12, transcendentals=0
        ),
        name="plane_sum",
    )(where, own, *received)


def final_kernel(parts, columns, p_chunk, where_ref, *refs):
    own, width = window_of(columns, parts)
    out_ref = refs[-1]
    me = where_ref[2]
    first = jnp.minimum(me * own // LANES * LANES, columns - width)
    shift = me * own - first
    for j in range(CHUNKS):
        group = refs[j * parts : (j + 1) * parts]
        value = group[0][...]
        for ref in group[1:]:
            value = value + ref[...].astype(jnp.float32)
        value = pltpu.roll(value, jnp.where(shift == 0, 0, width - shift), 1)[:, :own]
        u_own = out_ref.shape[2]
        value = value.reshape(2, p_chunk, u_own, own)
        out_ref[:, j * p_chunk : (j + 1) * p_chunk] = value


def final_sum(parts, columns, p_own, u_own, where, groups):
    own, _ = window_of(columns, parts)
    flat = [x for group in groups for x in group]
    vmem = pl.BlockSpec(memory_space=pltpu.VMEM)
    return pl.pallas_call(
        functools.partial(final_kernel, parts, columns, p_own // CHUNKS),
        out_shape=jax.ShapeDtypeStruct((2, p_own, u_own, own), jnp.float32),
        in_specs=[pl.BlockSpec(memory_space=pltpu.SMEM)] + [vmem] * len(flat),
        out_specs=vmem,
        name="final_sum",
    )(where, *flat)


def swap(size, bit):
    return [(i, i ^ bit) for i in range(size)]


def local(integrals, bra_rows, ket_rows, block_count, pair_count):
    columns = integrals.shape[3]
    general, active = bra_rows.shape[3], ket_rows.shape[3]
    ao_size = lax.axis_size("ao")
    gen_size = lax.axis_size("gen")
    act_size = lax.axis_size("act")
    where = jnp.stack(
        [lax.axis_index("gen"), lax.axis_index("act"), lax.axis_index("ao")]
    ).astype(jnp.int32)
    bra = jnp.swapaxes(bra_rows, 2, 3)
    ket = jnp.swapaxes(ket_rows, 2, 3)
    p_own, u_own = general // gen_size, active // act_size
    block = 2 * (p_own // CHUNKS) * u_own
    groups = []
    for chunk in range(CHUNKS):
        keep, send = products(
            chunk, (gen_size, act_size), block_count, pair_count, where, bra, ket, integrals
        )
        got = lax.ppermute(send, "gen", swap(gen_size, 1))
        both = keep + got.astype(jnp.float32)
        received = []
        index = 0
        for g in range(0, gen_size, 2):
            for a in range(act_size):
                piece = both[index * block : (index + 1) * block]
                index += 1
                if g == 0 and a == 0:
                    own = piece
                    continue
                pairs = [
                    (i * act_size + k, (i ^ g) * act_size + (k ^ a))
                    for i in range(gen_size)
                    for k in range(act_size)
                ]
                received.append(lax.ppermute(piece.astype(jnp.bfloat16), ("gen", "act"), pairs))
        if ao_size <= 4:
            windows = plane_sum(ao_size, where, own, received)
            group = [windows[0]]
            for k in range(1, ao_size):
                group.append(lax.ppermute(windows[k], "ao", swap(ao_size, k)))
            groups.append(group)
        else:
            total = own
            for x in received:
                total = total + x.astype(jnp.float32)
            total = total.reshape(block, ao_size, columns // ao_size)
            total = jnp.swapaxes(total, 0, 1).reshape(ao_size * block, columns // ao_size)
            total = lax.psum_scatter(total, "ao", scatter_dimension=0, tiled=True)
            groups.append(total.reshape(2, p_own // CHUNKS, u_own, columns // ao_size))
    if ao_size <= 4:
        return final_sum(ao_size, columns, p_own, u_own, where, groups)
    return jnp.concatenate(groups, axis=1)


def solution(mesh):
    spec = P(("ao", "gen", "act"), None, None, None)
    count = P(("ao", "gen", "act"))
    return jax.shard_map(
        local,
        mesh=mesh,
        in_specs=(spec, spec, spec, count, count),
        out_specs=P(None, "gen", "act", "ao"),
        check_vma=False,
    )
```

```python
import functools

import jax
import jax.numpy as jnp
from jax import lax
from jax.experimental import pallas as pl
from jax.experimental.pallas import tpu as pltpu
from jax.sharding import PartitionSpec as P


LANES = 128
GRAIN = 16
STEP = 2
GRANT = 48 * 2**20
PARTS = (1, 1)


def parts_of(p_own):
    if p_own % sum(PARTS):
        return (p_own,)
    return tuple(p_own // sum(PARTS) * part for part in PARTS)


def blocks_of(dims, chunk):
    general, _, gen_size, act_size = dims
    parts = parts_of(general // gen_size)
    p_from = sum(parts[:chunk])
    return [
        (g, a, p_from, p_from + parts[chunk])
        for parity in (1, 0)
        for g in range(parity, gen_size, 2)
        for a in range(act_size)
    ]


def make_weights(dims, chunk, t, column, bra_pack, ket_pack, weights):
    general, active, gen_size, act_size = dims
    p_own, u_own = general // gen_size, active // act_size
    me_gen, me_act = lax.axis_index("gen"), lax.axis_index("act")
    left, right = slice(column, column + LANES), slice(column + LANES, column + 2 * LANES)
    row = 0
    for g, a, p_from, p_to in blocks_of(dims, chunk):
        p_first = (me_gen ^ g) * p_own
        u_first = pl.multiple_of((me_act ^ a) * u_own, 8)
        ket_re = ket_pack[t, pl.ds(u_first, u_own), :]
        ket_im = ket_pack[t, pl.ds(active + u_first, u_own), :]
        real, imag = [], []
        for p in range(p_from, p_to):
            bra_re = bra_pack[t, pl.ds(p_first + p, 1), :]
            bra_im = bra_pack[t, pl.ds(general + p_first + p, 1), :]
            real.append(bra_re * ket_re + bra_im * ket_im)
            imag.append(bra_re * ket_im - bra_im * ket_re)
        rows = 2 * (p_to - p_from) * u_own
        first = jnp.concatenate(real + imag, axis=0).astype(jnp.bfloat16)
        second = jnp.concatenate([-x for x in imag] + real, axis=0).astype(jnp.bfloat16)
        weights[row : row + rows, left] = first
        weights[row : row + rows, right] = second
        row += rows


def product_kernel(dims, chunk, blocks, width, counts_ref, *refs):
    outs = 1 + len(blocks_of(dims, chunk)) // 2
    if chunk == 0:
        rows_ref, ints_ref = refs[:2]
        results = refs[2 : 2 + outs]
        bra_pack, ket_pack = refs[2 + outs : 4 + outs]
    else:
        bra_pack, ket_pack, ints_ref = refs[:3]
        results = refs[3 : 3 + outs]
    packed, weights, acc, offsets, sems = refs[-5:]
    general = dims[0]
    live = counts_ref[blocks]

    def rows_of(b):
        return (counts_ref[b] + GRAIN - 1) // GRAIN * GRAIN

    pieces = []
    size = width
    while size >= GRAIN:
        pieces.append(size)
        size //= 2

    def copies(b, act):
        rows = rows_of(b)
        start = pl.multiple_of(offsets[b], GRAIN)
        for piece in pieces:
            @pl.when((rows & piece) != 0)
            def _():
                first = pl.multiple_of(rows & ~(2 * piece - 1), GRAIN)
                copy = pltpu.make_async_copy(
                    ints_ref.at[b, :, pl.ds(first, piece), :],
                    packed.at[:, pl.ds(start + first, piece), :],
                    sems.at[b],
                )
                act(copy)

    def place(b, total):
        offsets[b] = total
        copies(b, lambda c: c.start())
        return total + rows_of(b)

    total = lax.fori_loop(0, live, place, 0)
    steps = (total + STEP * LANES - 1) // (STEP * LANES)

    def clear(i, _):
        row = pl.multiple_of(total + i * GRAIN, GRAIN)
        packed[:, pl.ds(row, GRAIN), :] = jnp.zeros((2, GRAIN, packed.shape[2]), packed.dtype)
        return 0

    lax.fori_loop(0, (steps * STEP * LANES - total) // GRAIN, clear, 0)

    if chunk == 0:
        @pl.loop(0, steps * STEP + 1)
        def _(t):
            bra_pack[t] = jnp.zeros(bra_pack.shape[1:], jnp.float32)
            ket_pack[t] = jnp.zeros(ket_pack.shape[1:], jnp.float32)

        lane = lax.broadcasted_iota(jnp.int32, (1, LANES), 1)
        for b in range(blocks):
            start = jnp.where(b < live, offsets[b], 0)
            rows = jnp.where(b < live, counts_ref[b], 0)
            tile = start // LANES
            turn = start % LANES
            both = rows_ref[b].astype(jnp.float32)
            for first, last, target in ((0, general, bra_pack), (general, both.shape[1], ket_pack)):
                value = both[:, first:last].reshape(target.shape[1:])
                value = pltpu.roll(jnp.where(lane < rows, value, 0.0), turn, 1)
                target[tile] += jnp.where(lane >= turn, value, 0.0)
                target[tile + 1] += jnp.where(lane < turn, value, 0.0)

    acc[...] = jnp.zeros_like(acc)

    def product(i, ready):
        for k in range(STEP):
            make_weights(
                dims, chunk, i * STEP + k, 2 * LANES * k, bra_pack, ket_pack, weights
            )

        def pending(b):
            start = offsets[jnp.minimum(b, blocks - 1)]
            return jnp.logical_and(b < live, start < (i + 1) * STEP * LANES)

        def arrive(b):
            copies(b, lambda c: c.wait())
            return b + 1

        ready = lax.while_loop(pending, arrive, ready)
        values = []
        for k in range(STEP):
            first = pl.multiple_of((i * STEP + k) * LANES, LANES)
            values.append(packed[0, pl.ds(first, LANES), :])
            values.append(packed[1, pl.ds(first, LANES), :])
        values = jnp.concatenate(values, axis=0)
        return jnp.dot(weights[...], values, preferred_element_type=jnp.float32), ready

    def step(i, ready):
        value, ready = product(i, ready)
        acc[...] += value
        return ready

    ready = lax.fori_loop(0, steps - 1, step, 0)
    value, _ = product(steps - 1, ready)
    value = acc[...] + value
    row = 0
    for result in results:
        result[...] = value[row : row + result.shape[0]].astype(result.dtype)
        row += result.shape[0]


SMEM = pl.BlockSpec(memory_space=pltpu.SMEM)
VMEM = pl.BlockSpec(memory_space=pltpu.VMEM)
HBM = pl.BlockSpec(memory_space=pltpu.HBM)


def products(dims, chunk, counts, operands, integrals):
    general, active, _, act_size = dims
    blocks, _, width, columns = integrals.shape
    u_own = active // act_size
    tiles = -(-blocks * width // (STEP * LANES)) * STEP
    sizes = [2 * (p_to - p_from) * u_own for _, _, p_from, p_to in blocks_of(dims, chunk)]
    rows = sum(sizes)
    outs = [jax.ShapeDtypeStruct((rows // 2, columns), jnp.bfloat16)]
    outs += [
        jax.ShapeDtypeStruct((size, columns), jnp.float32) for size in sizes[len(sizes) // 2 :]
    ]
    if chunk == 0:
        outs += [
            jax.ShapeDtypeStruct((tiles + 1, 2 * general, LANES), jnp.float32),
            jax.ShapeDtypeStruct((tiles + 1, 2 * active, LANES), jnp.float32),
        ]
    return pl.pallas_call(
        functools.partial(product_kernel, dims, chunk, blocks, width),
        out_shape=outs,
        in_specs=[SMEM] + [VMEM] * len(operands) + [HBM],
        out_specs=[VMEM] * len(outs),
        scratch_shapes=[
            pltpu.VMEM((2, tiles * LANES, columns), jnp.bfloat16),
            pltpu.VMEM((rows, 2 * STEP * LANES), jnp.bfloat16),
            pltpu.VMEM((rows, columns), jnp.float32),
            pltpu.SMEM((blocks,), jnp.int32),
            pltpu.SemaphoreType.DMA((blocks,)),
        ],
        compiler_params=pltpu.CompilerParams(vmem_limit_bytes=GRANT),
        cost_estimate=pl.CostEstimate(
            flops=rows * columns * 2 * blocks * LANES,
            bytes_accessed=rows * columns * 3,
            transcendentals=0,
        ),
    )(counts, *operands, integrals)


def window_of(columns, parts):
    own = columns // parts
    starts = [own * a // LANES * LANES for a in range(parts)]
    ends = [-(-own * (a + 1) // LANES) * LANES for a in range(parts)]
    width = max(e - s for s, e in zip(starts, ends))
    return own, width, [min(s, columns - width) for s in starts]


def choose(index, values):
    result = values[0]
    for i in range(1, len(values)):
        result = jnp.where(index == i, values[i], result)
    return result


def swap(size, bit):
    return [(i, i ^ bit) for i in range(size)]


def local(integrals, bra_rows, ket_rows, block_count, pair_count):
    columns = integrals.shape[3]
    general, active = bra_rows.shape[3], ket_rows.shape[3]
    ao_size = lax.axis_size("ao")
    gen_size = lax.axis_size("gen")
    act_size = lax.axis_size("act")
    me_ao = lax.axis_index("ao")
    bra = jnp.swapaxes(bra_rows, 2, 3)
    ket = jnp.swapaxes(ket_rows, 2, 3)
    p_own, u_own = general // gen_size, active // act_size
    dims = (general, active, gen_size, act_size)
    counts = jnp.concatenate([pair_count, block_count])
    operands = (jnp.concatenate([bra, ket], axis=2),)
    own, width, starts = window_of(columns, ao_size)
    outs = []
    kept = gen_size // 2 * act_size
    for chunk, part in enumerate(parts_of(p_own)):
        block = 2 * part * u_own
        send, *keep = products(dims, chunk, counts, operands, integrals)
        if chunk == 0:
            operands = tuple(keep[kept:])
        got = lax.ppermute(send, "gen", swap(gen_size, 1))
        index = 0
        for g in range(0, gen_size, 2):
            for a in range(act_size):
                piece = keep[index] + got[index * block : (index + 1) * block].astype(jnp.float32)
                index += 1
                if g == 0 and a == 0:
                    total = piece
                    continue
                pairs = [
                    (i * act_size + k, (i ^ g) * act_size + (k ^ a))
                    for i in range(gen_size)
                    for k in range(act_size)
                ]
                low = piece.astype(jnp.bfloat16)
                arrived = lax.ppermute(low, ("gen", "act"), pairs)
                total = total + arrived.astype(jnp.float32)
        if ao_size <= 4:
            windows = [total[:, s : s + width] for s in starts]
            value = choose(me_ao, windows)
            for k in range(1, ao_size):
                cut = choose(me_ao ^ k, windows).astype(jnp.bfloat16)
                arrived = lax.ppermute(cut, "ao", swap(ao_size, k))
                value = value + arrived.astype(jnp.float32)
            shifts = [own * a - starts[a] for a in range(ao_size)]
            value = choose(me_ao, [value[:, s : s + own] for s in shifts])
        else:
            total = total.reshape(block, ao_size, own)
            total = jnp.swapaxes(total, 0, 1).reshape(ao_size * block, own)
            value = lax.psum_scatter(total, "ao", scatter_dimension=0, tiled=True)
        outs.append(value.reshape(2, part, u_own, own))
    return jnp.concatenate(outs, axis=1)


def swap(size, bit):
    return [(i, i ^ bit) for i in range(size)]


def solution(mesh):
    spec = P(("ao", "gen", "act"), None, None, None)
    count = P(("ao", "gen", "act"))

    def program(integrals, bra_rows, ket_rows, block_count, pair_count):
        mapped = jax.shard_map(
            local,
            mesh=mesh,
            in_specs=(spec, spec, spec, count, count),
            out_specs=P(None, "gen", "act", "ao"),
            check_vma=False,
        )
        return mapped(integrals, bra_rows, ket_rows, block_count, pair_count)

    return program
```

```python
import functools

import jax
import jax.numpy as jnp
from jax import lax
from jax.experimental import pallas as pl
from jax.experimental.pallas import tpu as pltpu
from jax.sharding import PartitionSpec as P


LANES = 128
GRAIN = 16
STEP = 2
GRANT = 48 * 2**20
SMALL = 4 * 2**20
PARTS = (1, 1)


def parts_of(p_own):
    if p_own % sum(PARTS):
        return (p_own,)
    return tuple(p_own // sum(PARTS) * part for part in PARTS)


STAGES = (
    ("x", ((0, 1, 0), (1, 1, 0))),
    ("y", ((1, 0, 1), (1, 1, 1))),
    ("xy", ((1, 0, 0),)),
    ("yx", ((0, 1, 1),)),
    ("re", ((0, 0, 0),)),
    ("im", ((0, 0, 1),)),
)


def rows_of_stages(dims, chunk):
    general, active, gen_size, act_size = dims
    size = parts_of(general // gen_size)[chunk] * (active // act_size)
    found, row = {}, 0
    for name, members in STAGES:
        found[name] = (row, row + size * len(members))
        row += size * len(members)
    return found, row


def make_weights(dims, chunk, t, column, bra_pack, ket_pack, weights):
    general, active, gen_size, act_size = dims
    p_own, u_own = general // gen_size, active // act_size
    parts = parts_of(p_own)
    p_from = sum(parts[:chunk])
    size = parts[chunk] * u_own
    order = [member for _, members in STAGES for member in members]
    me_gen, me_act = lax.axis_index("gen"), lax.axis_index("act")
    left, right = slice(column, column + LANES), slice(column + LANES, column + 2 * LANES)
    for core in (1, 0):
        for q in range(gen_size // 2):
            for a in range(act_size):
                p_first = (me_gen ^ (2 * q + core)) * p_own + p_from
                u_first = pl.multiple_of((me_act ^ a) * u_own, 8)
                ket_re = ket_pack[t, pl.ds(u_first, u_own), :]
                ket_im = ket_pack[t, pl.ds(active + u_first, u_own), :]
                real, imag = [], []
                for p in range(parts[chunk]):
                    bra_re = bra_pack[t, pl.ds(p_first + p, 1), :]
                    bra_im = bra_pack[t, pl.ds(general + p_first + p, 1), :]
                    real.append(bra_re * ket_re + bra_im * ket_im)
                    imag.append(bra_re * ket_im - bra_im * ket_re)
                real = jnp.concatenate(real, axis=0)
                imag = jnp.concatenate(imag, axis=0)
                real_low = real.astype(jnp.bfloat16)
                base = (1 - core) * len(order) * size
                row = base + order.index((q, a, 0)) * size
                weights[row : row + size, left] = real_low
                weights[row : row + size, right] = (-imag).astype(jnp.bfloat16)
                row = base + order.index((q, a, 1)) * size
                weights[row : row + size, left] = imag.astype(jnp.bfloat16)
                weights[row : row + size, right] = real_low


def product_kernel(dims, chunk, blocks, width, counts_ref, *refs):
    outs = 1 + len(STAGES)
    if chunk == 0:
        rows_ref, ints_ref = refs[:2]
        results = refs[2 : 2 + outs]
        bra_pack, ket_pack = refs[2 + outs : 4 + outs]
    else:
        bra_pack, ket_pack, ints_ref = refs[:3]
        results = refs[3 : 3 + outs]
    packed, weights, acc, offsets, sems = refs[-5:]
    general = dims[0]
    live = counts_ref[blocks]

    def rows_of(b):
        return (counts_ref[b] + GRAIN - 1) // GRAIN * GRAIN

    pieces = []
    size = width
    while size >= GRAIN:
        pieces.append(size)
        size //= 2

    def copies(b, act):
        rows = rows_of(b)
        start = pl.multiple_of(offsets[b], GRAIN)
        for piece in pieces:
            @pl.when((rows & piece) != 0)
            def _():
                first = pl.multiple_of(rows & ~(2 * piece - 1), GRAIN)
                copy = pltpu.make_async_copy(
                    ints_ref.at[b, :, pl.ds(first, piece), :],
                    packed.at[:, pl.ds(start + first, piece), :],
                    sems.at[b],
                )
                act(copy)

    def place(b, total):
        offsets[b] = total
        copies(b, lambda c: c.start())
        return total + rows_of(b)

    total = lax.fori_loop(0, live, place, 0)
    steps = (total + STEP * LANES - 1) // (STEP * LANES)

    def clear(i, _):
        row = pl.multiple_of(total + i * GRAIN, GRAIN)
        packed[:, pl.ds(row, GRAIN), :] = jnp.zeros((2, GRAIN, packed.shape[2]), packed.dtype)
        return 0

    lax.fori_loop(0, (steps * STEP * LANES - total) // GRAIN, clear, 0)

    if chunk == 0:
        @pl.loop(0, steps * STEP + 1)
        def _(t):
            bra_pack[t] = jnp.zeros(bra_pack.shape[1:], jnp.float32)
            ket_pack[t] = jnp.zeros(ket_pack.shape[1:], jnp.float32)

        lane = lax.broadcasted_iota(jnp.int32, (1, LANES), 1)
        for b in range(blocks):
            start = jnp.where(b < live, offsets[b], 0)
            rows = jnp.where(b < live, counts_ref[b], 0)
            tile = start // LANES
            turn = start % LANES
            both = rows_ref[b].astype(jnp.float32)
            for first, last, target in ((0, general, bra_pack), (general, both.shape[1], ket_pack)):
                value = both[:, first:last].reshape(target.shape[1:])
                value = pltpu.roll(jnp.where(lane < rows, value, 0.0), turn, 1)
                target[tile] += jnp.where(lane >= turn, value, 0.0)
                target[tile + 1] += jnp.where(lane < turn, value, 0.0)

    acc[...] = jnp.zeros_like(acc)

    def product(i, ready):
        for k in range(STEP):
            make_weights(
                dims, chunk, i * STEP + k, 2 * LANES * k, bra_pack, ket_pack, weights
            )

        def pending(b):
            start = offsets[jnp.minimum(b, blocks - 1)]
            return jnp.logical_and(b < live, start < (i + 1) * STEP * LANES)

        def arrive(b):
            copies(b, lambda c: c.wait())
            return b + 1

        ready = lax.while_loop(pending, arrive, ready)
        values = []
        for k in range(STEP):
            first = pl.multiple_of((i * STEP + k) * LANES, LANES)
            values.append(packed[0, pl.ds(first, LANES), :])
            values.append(packed[1, pl.ds(first, LANES), :])
        values = jnp.concatenate(values, axis=0)
        return jnp.dot(weights[...], values, preferred_element_type=jnp.float32), ready

    def step(i, ready):
        value, ready = product(i, ready)
        acc[...] += value
        return ready

    ready = lax.fori_loop(0, steps - 1, step, 0)
    value, _ = product(steps - 1, ready)
    value = acc[...] + value
    row = 0
    for result in results:
        result[...] = value[row : row + result.shape[0]].astype(result.dtype)
        row += result.shape[0]


SMEM = pl.BlockSpec(memory_space=pltpu.SMEM)
VMEM = pl.BlockSpec(memory_space=pltpu.VMEM)
HBM = pl.BlockSpec(memory_space=pltpu.HBM)


def products(dims, chunk, counts, operands, integrals):
    general, active, _, _ = dims
    blocks, _, width, columns = integrals.shape
    tiles = -(-blocks * width // (STEP * LANES)) * STEP
    ranges, half = rows_of_stages(dims, chunk)
    rows = 2 * half
    outs = [jax.ShapeDtypeStruct((half, columns), jnp.bfloat16)]
    outs += [
        jax.ShapeDtypeStruct((last - first, columns), jnp.float32)
        for first, last in ranges.values()
    ]
    if chunk == 0:
        outs += [
            jax.ShapeDtypeStruct((tiles + 1, 2 * general, LANES), jnp.float32),
            jax.ShapeDtypeStruct((tiles + 1, 2 * active, LANES), jnp.float32),
        ]
    return pl.pallas_call(
        functools.partial(product_kernel, dims, chunk, blocks, width),
        out_shape=outs,
        in_specs=[SMEM] + [VMEM] * len(operands) + [HBM],
        out_specs=[VMEM] * len(outs),
        scratch_shapes=[
            pltpu.VMEM((2, tiles * LANES, columns), jnp.bfloat16),
            pltpu.VMEM((rows, 2 * STEP * LANES), jnp.bfloat16),
            pltpu.VMEM((rows, columns), jnp.float32),
            pltpu.SMEM((blocks,), jnp.int32),
            pltpu.SemaphoreType.DMA((blocks,)),
        ],
        compiler_params=pltpu.CompilerParams(vmem_limit_bytes=GRANT),
        cost_estimate=pl.CostEstimate(
            flops=rows * columns * 2 * blocks * LANES,
            bytes_accessed=rows * columns * 3,
            transcendentals=0,
        ),
    )(counts, *operands, integrals)


def window_of(columns, parts):
    own = columns // parts
    starts = [own * a // LANES * LANES for a in range(parts)]
    ends = [-(-own * (a + 1) // LANES) * LANES for a in range(parts)]
    width = max(e - s for s, e in zip(starts, ends))
    return own, width, [min(s, columns - width) for s in starts]


def small(kernel, outs, *operands):
    return pl.pallas_call(
        kernel,
        out_shape=outs,
        in_specs=[VMEM] * len(operands),
        out_specs=jax.tree.map(lambda _: VMEM, outs),
        compiler_params=pltpu.CompilerParams(vmem_limit_bytes=SMALL),
        cost_estimate=pl.CostEstimate(
            flops=sum(x.size for x in operands),
            bytes_accessed=4 * sum(x.size for x in operands),
            transcendentals=0,
        ),
    )(*operands)


def total_call(kernel, outs, shape, *operands):
    scratch = [pltpu.VMEM(shape, jnp.float32)] if outs else []
    outs = outs or [jax.ShapeDtypeStruct(shape, jnp.float32)]
    return pl.pallas_call(
        kernel,
        out_shape=outs,
        in_specs=[VMEM] * len(operands),
        out_specs=[VMEM] * len(outs),
        scratch_shapes=scratch,
        compiler_params=pltpu.CompilerParams(vmem_limit_bytes=SMALL),
        cost_estimate=pl.CostEstimate(
            flops=sum(x.size for x in operands),
            bytes_accessed=4 * sum(x.size for x in operands),
            transcendentals=0,
        ),
    )(*operands)


def wide(ref, ranges, name):
    first, last = ranges[name]
    return ref[first:last].astype(jnp.float32)


def first_kernel(ranges, x_ref, y_ref, got_ref, x_out, y_out):
    x_out[...] = (x_ref[...] + wide(got_ref, ranges, "x")).astype(x_out.dtype)
    y_out[...] = (y_ref[...] + wide(got_ref, ranges, "y")).astype(y_out.dtype)


def second_kernel(ranges, xy_ref, yx_ref, got_ref, from_x, from_y, xy_out, yx_out):
    size = xy_ref.shape[0]
    for kept, name, arrived, out in (
        (xy_ref, "xy", from_x, xy_out), (yx_ref, "yx", from_y, yx_out)
    ):
        value = kept[...] + wide(got_ref, ranges, name) + arrived[size:].astype(jnp.float32)
        out[...] = value.astype(out.dtype)


def total_kernel(ranges, parts, re_ref, im_ref, got_ref, from_x, from_y, from_xy, from_yx, *outs):
    size = re_ref.shape[0]
    total = outs[-1]
    for row, kept, name, first, second in (
        (0, re_ref, "re", from_x, from_xy), (size, im_ref, "im", from_y, from_yx)
    ):
        value = kept[...] + wide(got_ref, ranges, name) + first[:size].astype(jnp.float32)
        total[row : row + size] = value + second[...].astype(jnp.float32)
    if parts:
        columns = total.shape[1]
        own, width, _ = window_of(columns, parts)
        me = lax.axis_index("ao")
        for k, out in enumerate(outs[:-1]):
            first = jnp.minimum((me ^ k) * own // LANES * LANES, columns - width)
            cut = total[:, pl.ds(pl.multiple_of(first, LANES), width)]
            out[...] = cut.astype(out.dtype)


def final_kernel(parts, columns, *refs):
    out_ref = refs[-1]
    own, width, _ = window_of(columns, parts)
    me = lax.axis_index("ao")
    first = jnp.minimum(me * own // LANES * LANES, columns - width)
    shift = me * own - first
    p_from = 0
    for j in range(len(refs) // parts):
        group = refs[j * parts : (j + 1) * parts]
        value = group[0][...]
        for ref in group[1:]:
            value = value + ref[...].astype(jnp.float32)
        value = pltpu.roll(value, jnp.where(shift == 0, 0, width - shift), 1)[:, :own]
        u_own = out_ref.shape[2]
        part = value.shape[0] // (2 * u_own)
        out_ref[:, p_from : p_from + part] = value.reshape(2, part, u_own, own)
        p_from += part


def swap(size, bit):
    return [(i, i ^ bit) for i in range(size)]


def local(integrals, bra_rows, ket_rows, block_count, pair_count):
    columns = integrals.shape[3]
    general, active = bra_rows.shape[3], ket_rows.shape[3]
    ao_size = lax.axis_size("ao")
    gen_size = lax.axis_size("gen")
    act_size = lax.axis_size("act")
    bra = jnp.swapaxes(bra_rows, 2, 3)
    ket = jnp.swapaxes(ket_rows, 2, 3)
    p_own, u_own = general // gen_size, active // act_size
    dims = (general, active, gen_size, act_size)
    counts = jnp.concatenate([pair_count, block_count])
    operands = (jnp.concatenate([bra, ket], axis=2),)
    own, width, _ = window_of(columns, ao_size)
    outs = []
    assert (gen_size, act_size) == (4, 2)
    for chunk, part in enumerate(parts_of(p_own)):
        block = 2 * part * u_own
        ranges, _ = rows_of_stages(dims, chunk)
        send, *keep = products(dims, chunk, counts, operands, integrals)
        if chunk == 0:
            operands = tuple(keep[len(ranges) :])
        got = lax.ppermute(send, "gen", swap(gen_size, 1))
        keep = dict(zip(ranges, keep))

        def move(value, axis, bit):
            return lax.ppermute(value, axis, swap(lax.axis_size(axis), bit))

        low = jax.ShapeDtypeStruct(keep["x"].shape, jnp.bfloat16)
        to_x, to_y = small(
            functools.partial(first_kernel, ranges), [low, low],
            keep["x"], keep["y"], got,
        )
        from_x, from_y = move(to_x, "act", 1), move(to_y, "gen", 2)
        low = jax.ShapeDtypeStruct(keep["xy"].shape, jnp.bfloat16)
        to_xy, to_yx = small(
            functools.partial(second_kernel, ranges), [low, low],
            keep["xy"], keep["yx"], got, from_x, from_y,
        )
        from_xy, from_yx = move(to_xy, "gen", 2), move(to_yx, "act", 1)
        parts = ao_size if ao_size <= 4 else 0
        if parts:
            totals = [
                jax.ShapeDtypeStruct((block, width), jnp.bfloat16 if k else jnp.float32)
                for k in range(parts)
            ]
        else:
            totals = []
        windows = total_call(
            functools.partial(total_kernel, ranges, parts), totals,
            (block, columns), keep["re"], keep["im"], got, from_x, from_y, from_xy, from_yx,
        )
        if parts:
            outs.append(windows[0])
            outs += [move(windows[k], "ao", k) for k in range(1, parts)]
        else:
            total = windows[0].reshape(block, ao_size, own)
            total = jnp.swapaxes(total, 0, 1).reshape(ao_size * block, own)
            value = lax.psum_scatter(total, "ao", scatter_dimension=0, tiled=True)
            outs.append(value.reshape(2, part, u_own, own))
    if parts:
        result = jax.ShapeDtypeStruct((2, p_own, u_own, own), jnp.float32)
        return small(functools.partial(final_kernel, parts, columns), result, *outs)
    return jnp.concatenate(outs, axis=1)


def solution(mesh):
    spec = P(("ao", "gen", "act"), None, None, None)
    count = P(("ao", "gen", "act"))

    def program(integrals, bra_rows, ket_rows, block_count, pair_count):
        mapped = jax.shard_map(
            local,
            mesh=mesh,
            in_specs=(spec, spec, spec, count, count),
            out_specs=P(None, "gen", "act", "ao"),
            check_vma=False,
        )
        return mapped(integrals, bra_rows, ket_rows, block_count, pair_count)

    return program
```

```python
import functools

import jax
import jax.numpy as jnp
from jax import lax
from jax.experimental import pallas as pl
from jax.experimental.pallas import tpu as pltpu
from jax.sharding import PartitionSpec as P


LANES = 128
GRAIN = 8
STEP = 2
VMEM_BYTES = 67043328
SLACK = 12*2**20
SMALL = 4 * 2**20
PARTS = (1, 1)


def parts_of(p_own):
    if p_own % sum(PARTS):
        return (p_own,)
    return tuple(p_own // sum(PARTS) * part for part in PARTS)


STAGES = (("one", ((1, 0), (1, 1))), ("two", ((0, 1),)), ("own", ((0, 0),)))


def rows_of_stages(dims, chunk):
    general, active, gen_size, act_size = dims
    size = 2 * parts_of(general // gen_size)[chunk] * (active // act_size)
    found, row = {}, 0
    for name, members in STAGES:
        found[name] = (row, row + size * len(members))
        row += size * len(members)
    return found, row


def halves_of(ranges, half):
    first = ranges["one"][1]
    return (0, first), (first, half)


def make_weights(dims, chunk, t, column, bra_pack, ket_pack, weights):
    general, active, gen_size, act_size = dims
    p_own, u_own = general // gen_size, active // act_size
    parts = parts_of(p_own)
    p_from = sum(parts[:chunk])
    size = parts[chunk] * u_own
    order = [member for _, members in STAGES for member in members]
    me_gen, me_act = lax.axis_index("gen"), lax.axis_index("act")
    left, right = slice(column, column + LANES), slice(column + LANES, column + 2 * LANES)
    row = 0
    for core in (1, 0):
        odd = (me_gen & 1) ^ core
        for first, second in order:
            q = jnp.where(odd == 1, first, second)
            a = jnp.where(odd == 1, second, first)
            p_first = (me_gen ^ (2 * q + core)) * p_own + p_from
            u_first = pl.multiple_of((me_act ^ a) * u_own, 8)
            ket_re = ket_pack[t, pl.ds(u_first, u_own), :]
            ket_im = ket_pack[t, pl.ds(active + u_first, u_own), :]
            real, imag = [], []
            for p in range(parts[chunk]):
                bra_re = bra_pack[t, pl.ds(p_first + p, 1), :]
                bra_im = bra_pack[t, pl.ds(general + p_first + p, 1), :]
                real.append(bra_re * ket_re + bra_im * ket_im)
                imag.append(bra_re * ket_im - bra_im * ket_re)
            real = jnp.concatenate(real, axis=0)
            imag = jnp.concatenate(imag, axis=0)
            real_low = real.astype(jnp.bfloat16)
            weights[row : row + size, left] = real_low
            weights[row : row + size, right] = (-imag).astype(jnp.bfloat16)
            row += size
            weights[row : row + size, left] = imag.astype(jnp.bfloat16)
            weights[row : row + size, right] = real_low
            row += size


def accumulate(dims, chunk, tiles, packed, bra_pack, ket_pack, weights, acc, results, arrive):
    def product(first, count, state):
        for k in range(count):
            make_weights(dims, chunk, first + k, 2 * LANES * k, bra_pack, ket_pack, weights)
        state = arrive(first + count, state)
        values = []
        for k in range(count):
            row = pl.multiple_of((first + k) * LANES, LANES)
            values.append(packed[0, pl.ds(row, LANES), :])
            values.append(packed[1, pl.ds(row, LANES), :])
        values = jnp.concatenate(values, axis=0)
        left = weights[:, : 2 * LANES * count]
        return jnp.dot(left, values, preferred_element_type=jnp.float32), state

    def step(i, state):
        value, state = product(i * STEP, STEP, state)
        acc[...] += value
        return state

    steps = (tiles - 1) // STEP

    def opening(state):
        value, state = product(0, STEP, state)
        acc[...] = value
        return state

    def empty(state):
        acc[...] = jnp.zeros_like(acc)
        return state

    state = lax.cond(steps > 0, opening, empty, 0)
    state = lax.fori_loop(1, steps, step, state)
    for count in range(1, STEP + 1):
        @pl.when(tiles - steps * STEP == count)
        def _():
            value, _ = product(steps * STEP, count, state)
            value = acc[...] + value
            row = 0
            for result in results:
                result[...] = value[row : row + result.shape[0]].astype(result.dtype)
                row += result.shape[0]


def head_kernel(dims, blocks, width, counts, rows_ref, ints_ref, *refs):
    *results, packed, bra_pack, ket_pack = refs[:-4]
    weights, acc, offsets, sems = refs[-4:]
    general = dims[0]
    live = counts[blocks]

    def rows_of(b):
        return (counts[b] + GRAIN - 1) // GRAIN * GRAIN

    pieces = []
    size = width
    while size >= GRAIN:
        pieces.append(size)
        size //= 2

    def copies(b, act):
        rows = rows_of(b)
        start = pl.multiple_of(offsets[b], GRAIN)
        for piece in pieces:
            @pl.when((rows & piece) != 0)
            def _():
                first = pl.multiple_of(rows & ~(2 * piece - 1), GRAIN)
                copy = pltpu.make_async_copy(
                    ints_ref.at[b, :, pl.ds(first, piece), :],
                    packed.at[:, pl.ds(start + first, piece), :],
                    sems.at[b],
                )
                act(copy)

    def place(b, total):
        offsets[b] = total
        copies(b, lambda c: c.start())
        return total + rows_of(b)

    total = lax.fori_loop(0, live, place, 0)
    tiles = (total + LANES - 1) // LANES

    def clear(i, _):
        row = pl.multiple_of(total + i * GRAIN, GRAIN)
        packed[:, pl.ds(row, GRAIN), :] = jnp.zeros((2, GRAIN, packed.shape[2]), packed.dtype)
        return 0

    lax.fori_loop(0, (tiles * LANES - total) // GRAIN, clear, 0)

    @pl.loop(0, tiles + 1)
    def _(t):
        bra_pack[t] = jnp.zeros(bra_pack.shape[1:], jnp.float32)
        ket_pack[t] = jnp.zeros(ket_pack.shape[1:], jnp.float32)

    lane = lax.broadcasted_iota(jnp.int32, (1, LANES), 1)
    for b in range(blocks):
        start = jnp.where(b < live, offsets[b], 0)
        rows = jnp.where(b < live, counts[b], 0)
        tile = start // LANES
        turn = start % LANES
        both = rows_ref[b].astype(jnp.float32)
        for first, last, target in ((0, general, bra_pack), (general, both.shape[1], ket_pack)):
            value = both[:, first:last].reshape(target.shape[1:])
            value = pltpu.roll(jnp.where(lane < rows, value, 0.0), turn, 1)
            target[tile] += jnp.where(lane >= turn, value, 0.0)
            target[tile + 1] += jnp.where(lane < turn, value, 0.0)

    def arrive(until, ready):
        def pending(b):
            start = offsets[jnp.minimum(b, blocks - 1)]
            return jnp.logical_and(b < live, start < until * LANES)

        def wait(b):
            copies(b, lambda c: c.wait())
            return b + 1

        return lax.while_loop(pending, wait, ready)

    accumulate(dims, 0, tiles, packed, bra_pack, ket_pack, weights, acc, results, arrive)


def tail_kernel(dims, chunk, blocks, counts, packed, bra_pack, ket_pack, *refs):
    *results, weights, acc = refs

    def add(b, total):
        return total + (counts[b] + GRAIN - 1) // GRAIN * GRAIN

    total = lax.fori_loop(0, counts[blocks], add, 0)
    accumulate(
        dims, chunk, (total + LANES - 1) // LANES, packed, bra_pack, ket_pack, weights, acc, results,
        lambda until, state: state,
    )


SMEM = pl.BlockSpec(memory_space=pltpu.SMEM)
VMEM = pl.BlockSpec(memory_space=pltpu.VMEM)
HBM = pl.BlockSpec(memory_space=pltpu.HBM)


def products(dims, chunk, counts, operands):
    general, active, _, _ = dims
    columns = operands[-1].shape[3] if chunk == 0 else operands[0].shape[2]
    blocks = counts.shape[0] - 1
    ranges, half = rows_of_stages(dims, chunk)
    rows = 2 * half
    outs = [
        jax.ShapeDtypeStruct((last - first, columns), jnp.bfloat16)
        for first, last in halves_of(ranges, half)
    ]
    outs += [
        jax.ShapeDtypeStruct((last - first, columns), jnp.float32)
        for first, last in ranges.values()
    ]
    out_specs = [VMEM] * len(outs)
    work = [
        pltpu.VMEM((rows, 2 * STEP * LANES), jnp.bfloat16),
        pltpu.VMEM((rows, columns), jnp.float32),
    ]
    cost = pl.CostEstimate(
        flops=rows * columns * 2 * blocks * LANES, bytes_accessed=rows * columns * 3, transcendentals=0
    )
    if chunk:
        return pl.pallas_call(
            functools.partial(tail_kernel, dims, chunk, blocks),
            out_shape=outs,
            in_specs=[SMEM, VMEM, VMEM, VMEM],
            out_specs=out_specs,
            scratch_shapes=work,
            compiler_params=pltpu.CompilerParams(vmem_limit_bytes=16 * 2**20),
            cost_estimate=cost,
        )(counts, *operands)
    _, integrals = operands
    width = integrals.shape[2]
    tiles = -(-blocks * width // LANES)
    outs += [
        jax.ShapeDtypeStruct((2, tiles * LANES, columns), jnp.bfloat16),
        jax.ShapeDtypeStruct((tiles + 1, 2 * general, LANES), jnp.float32),
        jax.ShapeDtypeStruct((tiles + 1, 2 * active, LANES), jnp.float32),
    ]
    grant = VMEM_BYTES - sum(x.size * x.dtype.itemsize for x in outs) - SLACK
    return pl.pallas_call(
        functools.partial(head_kernel, dims, blocks, width),
        out_shape=outs,
        in_specs=[SMEM, VMEM, HBM],
        out_specs=[VMEM] * len(outs),
        scratch_shapes=[
            *work,
            pltpu.SMEM((blocks,), jnp.int32),
            pltpu.SemaphoreType.DMA((blocks,)),
        ],
        compiler_params=pltpu.CompilerParams(vmem_limit_bytes=grant),
        cost_estimate=cost,
        name="products_0",
    )(counts, *operands)


def window_of(columns, parts):
    own = columns // parts
    starts = [own * a // LANES * LANES for a in range(parts)]
    ends = [-(-own * (a + 1) // LANES) * LANES for a in range(parts)]
    return own, max(e - s for s, e in zip(starts, ends))


def dense_rows(own, rows):
    full, rest = divmod(own, LANES)
    return full * rows + rows * rest // LANES


def small(kernel, outs, *operands):
    return pl.pallas_call(
        kernel,
        out_shape=outs,
        in_specs=[VMEM] * len(operands),
        out_specs=jax.tree.map(lambda _: VMEM, outs),
        compiler_params=pltpu.CompilerParams(vmem_limit_bytes=SMALL),
        cost_estimate=pl.CostEstimate(
            flops=sum(x.size for x in operands),
            bytes_accessed=4 * sum(x.size for x in operands),
            transcendentals=0,
        ),
    )(*operands)


def total_call(kernel, outs, shape, *operands):
    scratch = [pltpu.VMEM(shape, jnp.float32)] if outs else []
    outs = outs or [jax.ShapeDtypeStruct(shape, jnp.float32)]
    return pl.pallas_call(
        kernel,
        out_shape=outs,
        in_specs=[VMEM] * len(operands),
        out_specs=[VMEM] * len(outs),
        scratch_shapes=scratch,
        compiler_params=pltpu.CompilerParams(vmem_limit_bytes=SMALL),
        cost_estimate=pl.CostEstimate(
            flops=sum(x.size for x in operands),
            bytes_accessed=4 * sum(x.size for x in operands),
            transcendentals=0,
        ),
    )(*operands)


def wide(ref, ranges, name):
    first, last = ranges[name]
    base = ranges["one"][1] if name != "one" else 0
    first, last = first - base, last - base
    return ref[first:last].astype(jnp.float32)


def first_kernel(ranges, one_ref, got_ref, one_out):
    one_out[...] = (one_ref[...] + wide(got_ref, ranges, "one")).astype(one_out.dtype)


def second_kernel(ranges, two_ref, got_ref, from_one, two_out):
    size = two_ref.shape[0]
    value = two_ref[...] + wide(got_ref, ranges, "two") + from_one[size:].astype(jnp.float32)
    two_out[...] = value.astype(two_out.dtype)


def total_kernel(ranges, parts, own_ref, got_ref, from_one, from_two, *outs):
    total = outs[-1]
    value = own_ref[...] + wide(got_ref, ranges, "own")
    value = value + from_one[: own_ref.shape[0]].astype(jnp.float32)
    total[...] = value + from_two[...].astype(jnp.float32)
    if parts:
        rows, columns = total.shape
        own, width = window_of(columns, parts)
        full, rest = divmod(own, LANES)
        lane = lax.broadcasted_iota(jnp.int32, (1, LANES), 1)
        me = lax.axis_index("ao")
        for k, out in enumerate(outs[:-1]):
            first = jnp.minimum((me ^ k) * own // LANES * LANES, columns - width)
            shift = (me ^ k) * own - first
            cut = total[:, pl.ds(pl.multiple_of(first, LANES), width)]
            cut = pltpu.roll(cut, jnp.where(shift == 0, 0, width - shift), 1)
            parcels = [cut[:, j * LANES : (j + 1) * LANES] for j in range(full)]
            if rest:
                groups = LANES // rest
                size = rows // groups
                left = cut[:, full * LANES : (full + 1) * LANES]
                parcel = left[:size]
                for g in range(1, groups):
                    moved = pltpu.roll(left[g * size : (g + 1) * size], g * rest, 1)
                    parcel = jnp.where(lane >= g * rest, moved, parcel)
                parcels.append(parcel)
            out[...] = jnp.concatenate(parcels, axis=0).astype(out.dtype)


def final_kernel(parts, own, *refs):
    out_ref = refs[-1]
    u_own = out_ref.shape[2]
    full, rest = divmod(own, LANES)
    p_from = 0
    for j in range(len(refs) // parts):
        group = refs[j * parts : (j + 1) * parts]
        value = group[0][...]
        for ref in group[1:]:
            value = value + ref[...].astype(jnp.float32)
        rows = value.shape[0] * LANES // own
        pieces = [value[i * rows : (i + 1) * rows] for i in range(full)]
        if rest:
            left = value[full * rows :]
            turns = [left] + [
                pltpu.roll(left, LANES - g * rest, 1) for g in range(1, LANES // rest)
            ]
            pieces.append(jnp.concatenate(turns, axis=0))
        value = jnp.concatenate(pieces, axis=1)[:, :own]
        part = rows // (2 * u_own)
        out_ref[:, p_from : p_from + part] = value.reshape(2, part, u_own, own)
        p_from += part


def swap(size, bit):
    return [(i, i ^ bit) for i in range(size)]


def local(integrals, bra_rows, ket_rows, block_count, pair_count):
    columns = integrals.shape[3]
    general, active = bra_rows.shape[3], ket_rows.shape[3]
    ao_size = lax.axis_size("ao")
    gen_size = lax.axis_size("gen")
    act_size = lax.axis_size("act")
    bra = jnp.swapaxes(bra_rows, 2, 3)
    ket = jnp.swapaxes(ket_rows, 2, 3)
    p_own, u_own = general // gen_size, active // act_size
    dims = (general, active, gen_size, act_size)
    counts = jnp.concatenate([pair_count, block_count])
    operands = (jnp.concatenate([bra, ket], axis=2), integrals)
    own, _ = window_of(columns, ao_size)
    outs = []
    assert (gen_size, act_size) == (4, 2)
    for chunk, part in enumerate(parts_of(p_own)):
        block = 2 * part * u_own
        ranges, _ = rows_of_stages(dims, chunk)
        to_core, to_core_rest, *keep = products(dims, chunk, counts, operands)
        if chunk == 0:
            operands = tuple(keep[len(ranges) :])
        got = lax.ppermute(to_core, "gen", swap(gen_size, 1))
        rest = lax.ppermute(to_core_rest, "gen", swap(gen_size, 1))
        keep = dict(zip(ranges, keep))

        def move(value, axis, bit):
            return lax.ppermute(value, axis, swap(lax.axis_size(axis), bit))

        def cross(value, odd_first):
            def partner(g, k):
                return (g ^ 2, k) if g % 2 == odd_first else (g, k ^ 1)

            pairs = []
            for g in range(gen_size):
                for k in range(act_size):
                    to_g, to_k = partner(g, k)
                    pairs.append((g * act_size + k, to_g * act_size + to_k))
            return lax.ppermute(value, ("gen", "act"), pairs)

        to_one = small(
            functools.partial(first_kernel, ranges),
            jax.ShapeDtypeStruct(keep["one"].shape, jnp.bfloat16), keep["one"], got,
        )
        from_one = cross(to_one, 1)
        to_two = small(
            functools.partial(second_kernel, ranges),
            jax.ShapeDtypeStruct(keep["two"].shape, jnp.bfloat16), keep["two"], rest, from_one,
        )
        from_two = cross(to_two, 0)
        parts = ao_size if ao_size <= 4 else 0
        if parts:
            totals = [
                jax.ShapeDtypeStruct(
                    (dense_rows(own, block), LANES), jnp.bfloat16 if k else jnp.float32
                )
                for k in range(parts)
            ]
        else:
            totals = []
        windows = total_call(
            functools.partial(total_kernel, ranges, parts), totals,
            (block, columns), keep["own"], rest, from_one, from_two,
        )
        if parts:
            outs.append(windows[0])
            outs += [move(windows[k], "ao", k) for k in range(1, parts)]
        else:
            total = windows[0].reshape(block, ao_size, own)
            total = jnp.swapaxes(total, 0, 1).reshape(ao_size * block, own)
            value = lax.psum_scatter(total, "ao", scatter_dimension=0, tiled=True)
            outs.append(value.reshape(2, part, u_own, own))
    if parts:
        result = jax.ShapeDtypeStruct((2, p_own, u_own, own), jnp.float32)
        return small(functools.partial(final_kernel, parts, own), result, *outs)
    return jnp.concatenate(outs, axis=1)


def solution(mesh):
    spec = P(("ao", "gen", "act"), None, None, None)
    count = P(("ao", "gen", "act"))

    def program(integrals, bra_rows, ket_rows, block_count, pair_count):
        mapped = jax.shard_map(
            local,
            mesh=mesh,
            in_specs=(spec, spec, spec, count, count),
            out_specs=P(None, "gen", "act", "ao"),
            check_vma=False,
        )
        return mapped(integrals, bra_rows, ket_rows, block_count, pair_count)

    return program
```

```python
import functools

import jax
import jax.numpy as jnp
from jax import lax
from jax.experimental import pallas as pl
from jax.experimental.pallas import tpu as pltpu
from jax.sharding import PartitionSpec as P


LANES = 128
GRAIN = 8
STEP = 2
VMEM_BYTES = 67043328
SLACK = 12*2**20
SMALL = 4 * 2**20
STAGES = ((("far", 1, 1), ("near", 1, 0)), (("two", 0, 1), ("own", 0, 0)))


def parts_of(p_own):
    return (p_own // 2, p_own // 2) if p_own % 2 == 0 else (p_own,)


def make_weights(dims, wave, t, left, bra_pack, ket_pack, weights):
    general, active, gen_size, act_size = dims
    p_own, u_own = general // gen_size, active // act_size
    me_gen, me_act = lax.axis_index("gen"), lax.axis_index("act")
    right = left + 1
    row = 0
    for core in (1, 0):
        odd = (me_gen & 1) ^ core
        for _, first, second in STAGES[wave]:
            q = jnp.where(odd == 1, first, second)
            a = jnp.where(odd == 1, second, first)
            p_first = (me_gen ^ (2 * q + core)) * p_own
            u_first = pl.multiple_of((me_act ^ a) * u_own, 8)
            ket_re = ket_pack[t, pl.ds(u_first, u_own), :]
            ket_im = ket_pack[t, pl.ds(active + u_first, u_own), :]
            p_from = 0
            for part in parts_of(p_own):
                real, imag = [], []
                for p in range(p_from, p_from + part):
                    bra_re = bra_pack[t, pl.ds(p_first + p, 1), :]
                    bra_im = bra_pack[t, pl.ds(general + p_first + p, 1), :]
                    real.append(bra_re * ket_re + bra_im * ket_im)
                    imag.append(bra_re * ket_im - bra_im * ket_re)
                p_from += part
                size = part * u_own
                real = jnp.concatenate(real, axis=0)
                imag = jnp.concatenate(imag, axis=0)
                real_low = real.astype(jnp.bfloat16)
                weights[left, row : row + size] = real_low
                weights[right, row : row + size] = (-imag).astype(jnp.bfloat16)
                row += size
                weights[left, row : row + size] = imag.astype(jnp.bfloat16)
                weights[right, row : row + size] = real_low
                row += size


def accumulate(dims, chunk, tiles, packed, bra_pack, ket_pack, weights, acc, results, arrive):
    def product(first, count, state):
        for k in range(count):
            make_weights(dims, chunk, first + k, 2 * k, bra_pack, ket_pack, weights)
        state = arrive(first + count, state)
        values = []
        for k in range(count):
            row = pl.multiple_of((first + k) * LANES, LANES)
            values.append(packed[0, pl.ds(row, LANES), :])
            values.append(packed[1, pl.ds(row, LANES), :])
        values = jnp.concatenate(values, axis=0)
        left = jnp.concatenate([weights[k] for k in range(2 * count)], axis=1)
        return jnp.dot(left, values, preferred_element_type=jnp.float32), state

    def step(i, state):
        value, state = product(i * STEP, STEP, state)
        acc[...] += value
        return state

    steps = (tiles - 1) // STEP

    def opening(state):
        value, state = product(0, STEP, state)
        acc[...] = value
        return state

    def empty(state):
        acc[...] = jnp.zeros_like(acc)
        return state

    state = lax.cond(steps > 0, opening, empty, 0)
    state = lax.fori_loop(1, steps, step, state)
    for count in range(1, STEP + 1):
        @pl.when(tiles - steps * STEP == count)
        def _():
            value, _ = product(steps * STEP, count, state)
            value = acc[...] + value
            row = 0
            for result in results:
                result[...] = value[row : row + result.shape[0]].astype(result.dtype)
                row += result.shape[0]


def head_kernel(dims, blocks, width, rows_ref, ints_ref, *refs):
    *results, packed, bra_pack, ket_pack = refs[:-5]
    weights, acc, counts, offsets, sems = refs[-5:]
    general = dims[0]

    def rows_of(b):
        return (counts[b] + GRAIN - 1) // GRAIN * GRAIN

    pieces = []
    size = width
    while size >= GRAIN:
        pieces.append(size)
        size //= 2

    def pieced(b, rows, start, piece):
        first = pl.multiple_of(rows & ~(2 * piece - 1), GRAIN)
        return pltpu.make_async_copy(
            ints_ref.at[b, :, pl.ds(first, piece), :],
            packed.at[:, pl.ds(start + first, piece), :],
            sems.at[b],
        )

    total = 0
    for b in range(blocks):
        marks = rows_ref[b, 0, rows_ref.shape[2] - 8 :].astype(jnp.float32)
        counts[b] = jnp.max(marks).astype(jnp.int32)
        rows = rows_of(b)
        offsets[b] = total
        start = pl.multiple_of(total, GRAIN)
        for piece in pieces:
            @pl.when((rows & piece) != 0)
            def _():
                pieced(b, rows, start, piece).start()

        total = total + rows
    tiles = (total + LANES - 1) // LANES

    def clear(i, _):
        row = pl.multiple_of(total + i * GRAIN, GRAIN)
        packed[:, pl.ds(row, GRAIN), :] = jnp.zeros((2, GRAIN, packed.shape[2]), packed.dtype)
        return 0

    lax.fori_loop(0, (tiles * LANES - total) // GRAIN, clear, 0)

    @pl.loop(0, tiles + 1)
    def _(t):
        bra_pack[t] = jnp.zeros(bra_pack.shape[1:], jnp.float32)
        ket_pack[t] = jnp.zeros(ket_pack.shape[1:], jnp.float32)

    bra_pack[bra_pack.shape[0] - 1] = jnp.full(
        bra_pack.shape[1:], tiles.astype(jnp.float32), jnp.float32
    )
    lane = lax.broadcasted_iota(jnp.int32, (1, LANES), 1)
    for b in range(blocks):
        start = offsets[b]
        rows = counts[b]
        tile = start // LANES
        turn = start % LANES
        both = rows_ref[b].astype(jnp.float32)
        for first, last, target in ((0, general, bra_pack), (general, both.shape[1] - 8, ket_pack)):
            value = both[:, first:last].reshape(target.shape[1:])
            value = pltpu.roll(jnp.where(lane < rows, value, 0.0), turn, 1)
            target[tile] += jnp.where(lane >= turn, value, 0.0)
            target[tile + 1] += jnp.where(lane < turn, value, 0.0)

    def arrive(until, ready):
        def pending(b):
            start = offsets[jnp.minimum(b, blocks - 1)]
            return jnp.logical_and(b < blocks, start < jnp.minimum(until * LANES, total))

        def wait(b):
            rows = rows_of(b)
            start = pl.multiple_of(offsets[b], GRAIN)
            for piece in pieces:
                @pl.when((rows & piece) != 0)
                def _():
                    pieced(b, rows, start, piece).wait()

            return b + 1

        return lax.while_loop(pending, wait, ready)

    accumulate(dims, 0, tiles, packed, bra_pack, ket_pack, weights, acc, results, arrive)


def tail_kernel(dims, chunk, packed, bra_pack, ket_pack, *refs):
    *results, weights, acc = refs
    tiles = jnp.max(bra_pack[bra_pack.shape[0] - 1, :8]).astype(jnp.int32)
    accumulate(
        dims, chunk, tiles, packed, bra_pack, ket_pack, weights, acc, results,
        lambda until, state: state,
    )


SMEM = pl.BlockSpec(memory_space=pltpu.SMEM)
VMEM = pl.BlockSpec(memory_space=pltpu.VMEM)
HBM = pl.BlockSpec(memory_space=pltpu.HBM)


def products(dims, chunk, operands):
    general, active, gen_size, act_size = dims
    columns = operands[-1].shape[3] if chunk == 0 else operands[0].shape[2]
    blocks = operands[0].shape[0]
    blocks_rows = [2 * part * (active // act_size) for part in parts_of(general // gen_size)]
    half = sum(blocks_rows)
    rows = 2 * half * len(STAGES[chunk])
    outs = [jax.ShapeDtypeStruct((half, columns), jnp.bfloat16) for _ in STAGES[chunk]]
    outs += [
        jax.ShapeDtypeStruct((size, columns), jnp.float32)
        for _ in STAGES[chunk]
        for size in blocks_rows
    ]
    out_specs = [VMEM] * len(outs)
    work = [
        pltpu.VMEM((2 * STEP, rows, LANES), jnp.bfloat16),
        pltpu.VMEM((rows, columns), jnp.float32),
    ]
    cost = pl.CostEstimate(
        flops=rows * columns * 2 * blocks * LANES, bytes_accessed=rows * columns * 3, transcendentals=0
    )
    if chunk:
        return pl.pallas_call(
            functools.partial(tail_kernel, dims, chunk),
            out_shape=outs,
            in_specs=[VMEM, VMEM, VMEM],
            out_specs=out_specs,
            scratch_shapes=work,
            compiler_params=pltpu.CompilerParams(vmem_limit_bytes=16 * 2**20),
            cost_estimate=cost,
        )(*operands)
    _, integrals = operands
    width = integrals.shape[2]
    tiles = -(-blocks * width // LANES)
    outs += [
        jax.ShapeDtypeStruct((2, tiles * LANES, columns), jnp.bfloat16),
        jax.ShapeDtypeStruct((tiles + 2, 2 * general, LANES), jnp.float32),
        jax.ShapeDtypeStruct((tiles + 1, 2 * active, LANES), jnp.float32),
    ]
    grant = VMEM_BYTES - sum(x.size * x.dtype.itemsize for x in outs) - SLACK
    return pl.pallas_call(
        functools.partial(head_kernel, dims, blocks, width),
        out_shape=outs,
        in_specs=[VMEM, HBM],
        out_specs=[VMEM] * len(outs),
        scratch_shapes=[
            *work,
            pltpu.SMEM((blocks,), jnp.int32),
            pltpu.SMEM((blocks,), jnp.int32),
            pltpu.SemaphoreType.DMA((blocks,)),
        ],
        compiler_params=pltpu.CompilerParams(vmem_limit_bytes=grant),
        cost_estimate=cost,
        name="products_0",
    )(*operands)


def window_of(columns, parts):
    own = columns // parts
    starts = [own * a // LANES * LANES for a in range(parts)]
    ends = [-(-own * (a + 1) // LANES) * LANES for a in range(parts)]
    return own, max(e - s for s, e in zip(starts, ends))


def dense_rows(own, rows):
    full, rest = divmod(own, LANES)
    return full * rows + rows * rest // LANES


def small(kernel, outs, *operands):
    return pl.pallas_call(
        kernel,
        out_shape=outs,
        in_specs=[VMEM] * len(operands),
        out_specs=jax.tree.map(lambda _: VMEM, outs),
        compiler_params=pltpu.CompilerParams(vmem_limit_bytes=SMALL),
        cost_estimate=pl.CostEstimate(
            flops=sum(x.size for x in operands),
            bytes_accessed=4 * sum(x.size for x in operands),
            transcendentals=0,
        ),
    )(*operands)


def total_call(kernel, outs, shape, *operands):
    scratch = [pltpu.VMEM(shape, jnp.float32)] if outs else []
    outs = outs or [jax.ShapeDtypeStruct(shape, jnp.float32)]
    return pl.pallas_call(
        kernel,
        out_shape=outs,
        in_specs=[VMEM] * len(operands),
        out_specs=[VMEM] * len(outs),
        scratch_shapes=scratch,
        compiler_params=pltpu.CompilerParams(vmem_limit_bytes=SMALL),
        cost_estimate=pl.CostEstimate(
            flops=sum(x.size for x in operands),
            bytes_accessed=4 * sum(x.size for x in operands),
            transcendentals=0,
        ),
    )(*operands)


def far_kernel(*refs):
    *kept, got_ref, out = refs
    row = 0
    for ref in kept:
        last = row + ref.shape[0]
        value = ref[...] + got_ref[row:last].astype(jnp.float32)
        out[row:last] = value.astype(out.dtype)
        row = last


def near_kernel(row, kept_ref, got_ref, out):
    last = row + kept_ref.shape[0]
    out[...] = (kept_ref[...] + got_ref[row:last].astype(jnp.float32)).astype(out.dtype)


def two_kernel(row, kept_ref, got_ref, from_far, out):
    last = row + kept_ref.shape[0]
    value = kept_ref[...] + got_ref[row:last].astype(jnp.float32)
    out[...] = (value + from_far[row:last].astype(jnp.float32)).astype(out.dtype)


def total_kernel(row, parts, own_ref, got_ref, from_near, from_two, *outs):
    total = outs[-1]
    last = row + own_ref.shape[0]
    value = own_ref[...] + got_ref[row:last].astype(jnp.float32)
    total[...] = value + from_near[...].astype(jnp.float32) + from_two[...].astype(jnp.float32)
    if parts:
        rows, columns = total.shape
        own, width = window_of(columns, parts)
        full, rest = divmod(own, LANES)
        lane = lax.broadcasted_iota(jnp.int32, (1, LANES), 1)
        me = lax.axis_index("ao")
        for k, out in enumerate(outs[:-1]):
            first = jnp.minimum((me ^ k) * own // LANES * LANES, columns - width)
            shift = (me ^ k) * own - first
            cut = total[:, pl.ds(pl.multiple_of(first, LANES), width)]
            cut = pltpu.roll(cut, jnp.where(shift == 0, 0, width - shift), 1)
            parcels = [cut[:, j * LANES : (j + 1) * LANES] for j in range(full)]
            if rest:
                groups = LANES // rest
                size = rows // groups
                left = cut[:, full * LANES : (full + 1) * LANES]
                parcel = left[:size]
                for g in range(1, groups):
                    moved = pltpu.roll(left[g * size : (g + 1) * size], g * rest, 1)
                    parcel = jnp.where(lane >= g * rest, moved, parcel)
                parcels.append(parcel)
            out[...] = jnp.concatenate(parcels, axis=0).astype(out.dtype)


def final_kernel(parts, own, *refs):
    out_ref = refs[-1]
    u_own = out_ref.shape[2]
    full, rest = divmod(own, LANES)
    p_from = 0
    for j in range(len(refs) // parts):
        group = refs[j * parts : (j + 1) * parts]
        value = group[0][...]
        for ref in group[1:]:
            value = value + ref[...].astype(jnp.float32)
        rows = value.shape[0] * LANES // own
        pieces = [value[i * rows : (i + 1) * rows] for i in range(full)]
        if rest:
            left = value[full * rows :]
            turns = [left] + [
                pltpu.roll(left, LANES - g * rest, 1) for g in range(1, LANES // rest)
            ]
            pieces.append(jnp.concatenate(turns, axis=0))
        value = jnp.concatenate(pieces, axis=1)[:, :own]
        part = rows // (2 * u_own)
        out_ref[:, p_from : p_from + part] = value.reshape(2, part, u_own, own)
        p_from += part


def swap(size, bit):
    return [(i, i ^ bit) for i in range(size)]


def local(integrals, bra_rows, ket_rows, block_count, pair_count):
    columns = integrals.shape[3]
    general, active = bra_rows.shape[3], ket_rows.shape[3]
    ao_size = lax.axis_size("ao")
    gen_size = lax.axis_size("gen")
    act_size = lax.axis_size("act")
    bra = jnp.swapaxes(bra_rows, 2, 3)
    ket = jnp.swapaxes(ket_rows, 2, 3)
    p_own, u_own = general // gen_size, active // act_size
    dims = (general, active, gen_size, act_size)
    blocks, _, width, _ = integrals.shape
    assert width <= 256
    live = jnp.where(jnp.arange(blocks, dtype=jnp.int32) < block_count, pair_count, 0)
    tail = jnp.broadcast_to(live.astype(bra.dtype)[:, None, None, None], (blocks, 2, 8, width))
    operands = (jnp.concatenate([bra, ket, tail], axis=2), integrals)
    own, width = window_of(columns, ao_size)
    outs = []
    assert (gen_size, act_size) == (4, 2)
    sizes = [2 * part * u_own for part in parts_of(p_own)]
    low = [jax.ShapeDtypeStruct((size, columns), jnp.bfloat16) for size in sizes]

    def move(value, axis, bit):
        return lax.ppermute(value, axis, swap(lax.axis_size(axis), bit))

    def cross(value, odd_first):
        def partner(g, k):
            return (g ^ 2, k) if g % 2 == odd_first else (g, k ^ 1)

        pairs = []
        for g in range(gen_size):
            for k in range(act_size):
                to_g, to_k = partner(g, k)
                pairs.append((g * act_size + k, to_g * act_size + to_k))
        return lax.ppermute(value, ("gen", "act"), pairs)

    kept, got = {}, {}
    for wave, stages in enumerate(STAGES):
        made = list(products(dims, wave, operands))
        for name, _, _ in stages:
            got[name] = move(made.pop(0), "gen", 1)
        for name, _, _ in stages:
            kept[name] = [made.pop(0) for _ in sizes]
        if wave == 0:
            operands = tuple(made)
            whole = jax.ShapeDtypeStruct((sum(sizes), columns), jnp.bfloat16)
            value = small(far_kernel, whole, *kept["far"], got["far"])
            from_far = cross(value, 1)
    parts = ao_size if ao_size <= 4 else 0
    outs = []
    row = 0
    for j, size in enumerate(sizes):
        value = small(
            functools.partial(near_kernel, row), low[j],
            kept["near"][j], got["near"],
        )
        from_near = cross(value, 1)
        value = small(
            functools.partial(two_kernel, row), low[j],
            kept["two"][j], got["two"], from_far,
        )
        from_two = cross(value, 0)
        totals = [
            jax.ShapeDtypeStruct((dense_rows(own, size), LANES), jnp.bfloat16 if k else jnp.float32)
            for k in range(parts)
        ]
        pieces = total_call(
            functools.partial(total_kernel, row, parts), totals,
            (size, columns), kept["own"][j], got["own"], from_near, from_two,
        )
        row += size
        if parts:
            outs.append(pieces[0])
            outs += [move(pieces[k], "ao", k) for k in range(1, parts)]
        else:
            total = pieces[0].reshape(size, ao_size, own)
            total = jnp.swapaxes(total, 0, 1).reshape(ao_size * size, own)
            value = lax.psum_scatter(total, "ao", scatter_dimension=0, tiled=True)
            outs.append(value.reshape(2, -1, u_own, own))
    if parts:
        result = jax.ShapeDtypeStruct((2, p_own, u_own, own), jnp.float32)
        return small(functools.partial(final_kernel, parts, own), result, *outs)
    return jnp.concatenate(outs, axis=1)


def solution(mesh):
    spec = P(("ao", "gen", "act"), None, None, None)
    count = P(("ao", "gen", "act"))

    def program(integrals, bra_rows, ket_rows, block_count, pair_count):
        mapped = jax.shard_map(
            local,
            mesh=mesh,
            in_specs=(spec, spec, spec, count, count),
            out_specs=P(None, "gen", "act", "ao"),
            check_vma=False,
        )
        return mapped(integrals, bra_rows, ket_rows, block_count, pair_count)

    return program
```

```python
import functools

import jax
import jax.numpy as jnp
from jax import lax
from jax.experimental import pallas as pl
from jax.experimental.pallas import tpu as pltpu
from jax.sharding import PartitionSpec as P


LANES = 128
GRAIN = 8
STEP = 2
VMEM_BYTES = 67043328
SLACK = 12*2**20
SMALL = 4 * 2**20
STAGES = ((("far", 1, 1), ("near", 1, 0)), (("two", 0, 1), ("own", 0, 0)))


def parts_of(p_own):
    return (p_own // 2, p_own // 2) if p_own % 2 == 0 else (p_own,)


def make_weights(dims, wave, t, left, bra_pack, ket_pack, weights):
    general, active, gen_size, act_size = dims
    p_own, u_own = general // gen_size, active // act_size
    me_gen, me_act = lax.axis_index("gen"), lax.axis_index("act")
    right = left + 1
    row = 0
    for core in (1, 0):
        odd = (me_gen & 1) ^ core
        for _, first, second in STAGES[wave]:
            q = jnp.where(odd == 1, first, second)
            a = jnp.where(odd == 1, second, first)
            p_first = (me_gen ^ (2 * q + core)) * p_own
            u_first = pl.multiple_of((me_act ^ a) * u_own, 8)
            ket_re = ket_pack[t, pl.ds(u_first, u_own), :]
            ket_im = ket_pack[t, pl.ds(active + u_first, u_own), :]
            p_from = 0
            for part in parts_of(p_own):
                real, imag = [], []
                for p in range(p_from, p_from + part):
                    bra_re = bra_pack[t, pl.ds(p_first + p, 1), :]
                    bra_im = bra_pack[t, pl.ds(general + p_first + p, 1), :]
                    real.append(bra_re * ket_re + bra_im * ket_im)
                    imag.append(bra_re * ket_im - bra_im * ket_re)
                p_from += part
                size = part * u_own
                real = jnp.concatenate(real, axis=0)
                imag = jnp.concatenate(imag, axis=0)
                real_low = real.astype(jnp.bfloat16)
                weights[left, row : row + size] = real_low
                weights[right, row : row + size] = (-imag).astype(jnp.bfloat16)
                row += size
                weights[left, row : row + size] = imag.astype(jnp.bfloat16)
                weights[right, row : row + size] = real_low
                row += size


def accumulate(dims, chunk, tiles, packed, bra_pack, ket_pack, weights, acc, results, arrive):
    def product(first, count, state):
        for k in range(count):
            make_weights(dims, chunk, first + k, 2 * k, bra_pack, ket_pack, weights)
        state = arrive(first + count, state)
        values = []
        for k in range(count):
            row = pl.multiple_of((first + k) * LANES, LANES)
            values.append(packed[0, pl.ds(row, LANES), :])
            values.append(packed[1, pl.ds(row, LANES), :])
        values = jnp.concatenate(values, axis=0)
        left = jnp.concatenate([weights[k] for k in range(2 * count)], axis=1)
        return jnp.dot(left, values, preferred_element_type=jnp.float32), state

    def step(i, state):
        value, state = product(i * STEP, STEP, state)
        acc[...] += value
        return state

    steps = (tiles - 1) // STEP

    def opening(state):
        value, state = product(0, STEP, state)
        acc[...] = value
        return state

    def empty(state):
        acc[...] = jnp.zeros_like(acc)
        return state

    state = lax.cond(steps > 0, opening, empty, 0)
    state = lax.fori_loop(1, steps, step, state)
    for count in range(1, STEP + 1):
        @pl.when(tiles - steps * STEP == count)
        def _():
            value, _ = product(steps * STEP, count, state)
            value = acc[...] + value
            row = 0
            for result in results:
                result[...] = value[row : row + result.shape[0]].astype(result.dtype)
                row += result.shape[0]


def head_kernel(dims, blocks, width, rows_ref, ints_ref, *refs):
    *results, packed, bra_pack, ket_pack = refs[:-5]
    weights, acc, counts, offsets, sems = refs[-5:]
    general = dims[0]

    def rows_of(b):
        return (counts[b] + GRAIN - 1) // GRAIN * GRAIN

    pieces = []
    size = width
    while size >= GRAIN:
        pieces.append(size)
        size //= 2

    def pieced(b, rows, start, piece):
        first = pl.multiple_of(rows & ~(2 * piece - 1), GRAIN)
        return pltpu.make_async_copy(
            ints_ref.at[b, :, pl.ds(first, piece), :],
            packed.at[:, pl.ds(start + first, piece), :],
            sems.at[b],
        )

    total = 0
    for b in range(blocks):
        marks = rows_ref[b, 0, rows_ref.shape[2] - 8 :].astype(jnp.float32)
        counts[b] = jnp.max(marks).astype(jnp.int32)
        rows = rows_of(b)
        offsets[b] = total
        start = pl.multiple_of(total, GRAIN)
        for piece in pieces:
            @pl.when((rows & piece) != 0)
            def _():
                pieced(b, rows, start, piece).start()

        total = total + rows
    tiles = (total + LANES - 1) // LANES

    def clear(i, _):
        row = pl.multiple_of(total + i * GRAIN, GRAIN)
        packed[:, pl.ds(row, GRAIN), :] = jnp.zeros((2, GRAIN, packed.shape[2]), packed.dtype)
        return 0

    lax.fori_loop(0, (tiles * LANES - total) // GRAIN, clear, 0)

    @pl.loop(0, tiles + 1)
    def _(t):
        bra_pack[t] = jnp.zeros(bra_pack.shape[1:], jnp.float32)
        ket_pack[t] = jnp.zeros(ket_pack.shape[1:], jnp.float32)

    bra_pack[bra_pack.shape[0] - 1] = jnp.full(
        bra_pack.shape[1:], tiles.astype(jnp.float32), jnp.float32
    )
    lane = lax.broadcasted_iota(jnp.int32, (1, LANES), 1)
    for b in range(blocks):
        start = offsets[b]
        rows = counts[b]
        tile = start // LANES
        turn = start % LANES
        both = rows_ref[b].astype(jnp.float32)
        for first, last, target in ((0, general, bra_pack), (general, both.shape[1] - 8, ket_pack)):
            value = both[:, first:last].reshape(target.shape[1:])
            value = pltpu.roll(jnp.where(lane < rows, value, 0.0), turn, 1)
            target[tile] += jnp.where(lane >= turn, value, 0.0)
            target[tile + 1] += jnp.where(lane < turn, value, 0.0)

    def arrive(until, ready):
        def pending(b):
            start = offsets[jnp.minimum(b, blocks - 1)]
            return jnp.logical_and(b < blocks, start < jnp.minimum(until * LANES, total))

        def wait(b):
            rows = rows_of(b)
            start = pl.multiple_of(offsets[b], GRAIN)
            for piece in pieces:
                @pl.when((rows & piece) != 0)
                def _():
                    pieced(b, rows, start, piece).wait()

            return b + 1

        return lax.while_loop(pending, wait, ready)

    accumulate(dims, 0, tiles, packed, bra_pack, ket_pack, weights, acc, results, arrive)


def tail_kernel(dims, chunk, packed, bra_pack, ket_pack, *refs):
    *results, weights, acc = refs
    tiles = jnp.max(bra_pack[bra_pack.shape[0] - 1, :8]).astype(jnp.int32)
    accumulate(
        dims, chunk, tiles, packed, bra_pack, ket_pack, weights, acc, results,
        lambda until, state: state,
    )


SMEM = pl.BlockSpec(memory_space=pltpu.SMEM)
VMEM = pl.BlockSpec(memory_space=pltpu.VMEM)
HBM = pl.BlockSpec(memory_space=pltpu.HBM)


def products(dims, chunk, operands):
    general, active, gen_size, act_size = dims
    columns = operands[-1].shape[3] if chunk == 0 else operands[0].shape[2]
    blocks = operands[0].shape[0]
    blocks_rows = [2 * part * (active // act_size) for part in parts_of(general // gen_size)]
    half = sum(blocks_rows)
    rows = 2 * half * len(STAGES[chunk])
    outs = [jax.ShapeDtypeStruct((half, columns), jnp.bfloat16) for _ in STAGES[chunk]]
    outs += [
        jax.ShapeDtypeStruct((size, columns), jnp.float32)
        for _ in STAGES[chunk]
        for size in blocks_rows
    ]
    out_specs = [VMEM] * len(outs)
    work = [
        pltpu.VMEM((2 * STEP, rows, LANES), jnp.bfloat16),
        pltpu.VMEM((rows, columns), jnp.float32),
    ]
    cost = pl.CostEstimate(
        flops=rows * columns * 2 * blocks * LANES, bytes_accessed=rows * columns * 3, transcendentals=0
    )
    if chunk:
        return pl.pallas_call(
            functools.partial(tail_kernel, dims, chunk),
            out_shape=outs,
            in_specs=[VMEM, VMEM, VMEM],
            out_specs=out_specs,
            scratch_shapes=work,
            compiler_params=pltpu.CompilerParams(vmem_limit_bytes=16 * 2**20),
            cost_estimate=cost,
        )(*operands)
    _, integrals = operands
    width = integrals.shape[2]
    tiles = -(-blocks * width // LANES)
    outs += [
        jax.ShapeDtypeStruct((2, tiles * LANES, columns), jnp.bfloat16),
        jax.ShapeDtypeStruct((tiles + 2, 2 * general, LANES), jnp.float32),
        jax.ShapeDtypeStruct((tiles + 1, 2 * active, LANES), jnp.float32),
    ]
    grant = VMEM_BYTES - sum(x.size * x.dtype.itemsize for x in outs) - SLACK
    return pl.pallas_call(
        functools.partial(head_kernel, dims, blocks, width),
        out_shape=outs,
        in_specs=[VMEM, HBM],
        out_specs=[VMEM] * len(outs),
        scratch_shapes=[
            *work,
            pltpu.SMEM((blocks,), jnp.int32),
            pltpu.SMEM((blocks,), jnp.int32),
            pltpu.SemaphoreType.DMA((blocks,)),
        ],
        compiler_params=pltpu.CompilerParams(vmem_limit_bytes=grant),
        cost_estimate=cost,
        name="products_0",
    )(*operands)


def window_of(columns, parts):
    own = columns // parts
    starts = [own * a // LANES * LANES for a in range(parts)]
    ends = [-(-own * (a + 1) // LANES) * LANES for a in range(parts)]
    return own, max(e - s for s, e in zip(starts, ends))


def dense_rows(own, rows):
    full, rest = divmod(own, LANES)
    return full * rows + rows * rest // LANES


def small(kernel, outs, *operands):
    return pl.pallas_call(
        kernel,
        out_shape=outs,
        in_specs=[VMEM] * len(operands),
        out_specs=jax.tree.map(lambda _: VMEM, outs),
        compiler_params=pltpu.CompilerParams(vmem_limit_bytes=SMALL),
        cost_estimate=pl.CostEstimate(
            flops=sum(x.size for x in operands),
            bytes_accessed=4 * sum(x.size for x in operands),
            transcendentals=0,
        ),
    )(*operands)


def total_call(kernel, outs, shape, *operands):
    outs = outs or [jax.ShapeDtypeStruct(shape, jnp.float32)]
    return pl.pallas_call(
        kernel,
        out_shape=outs,
        in_specs=[VMEM] * len(operands),
        out_specs=[VMEM] * len(outs),
        compiler_params=pltpu.CompilerParams(vmem_limit_bytes=SMALL),
        cost_estimate=pl.CostEstimate(
            flops=sum(x.size for x in operands),
            bytes_accessed=4 * sum(x.size for x in operands),
            transcendentals=0,
        ),
    )(*operands)


def far_kernel(*refs):
    *kept, got_ref, out = refs
    row = 0
    for ref in kept:
        last = row + ref.shape[0]
        value = ref[...] + got_ref[row:last].astype(jnp.float32)
        out[row:last] = value.astype(out.dtype)
        row = last


def near_kernel(row, kept_ref, got_ref, out):
    last = row + kept_ref.shape[0]
    out[...] = (kept_ref[...] + got_ref[row:last].astype(jnp.float32)).astype(out.dtype)


def two_kernel(row, kept_ref, got_ref, from_far, out):
    last = row + kept_ref.shape[0]
    value = kept_ref[...] + got_ref[row:last].astype(jnp.float32)
    out[...] = (value + from_far[row:last].astype(jnp.float32)).astype(out.dtype)


def total_kernel(row, parts, shifts, own_ref, got_ref, from_near, from_two, *outs):
    rows, columns = own_ref.shape
    last = row + rows

    def sum_of(lanes):
        value = own_ref[:, lanes] + got_ref[row:last, lanes].astype(jnp.float32)
        value = value + from_near[:, lanes].astype(jnp.float32)
        return value + from_two[:, lanes].astype(jnp.float32)

    if not parts:
        outs[0][...] = sum_of(slice(None))
    if parts:
        own, width = window_of(columns, parts)
        full, rest = divmod(own, LANES)
        lane = lax.broadcasted_iota(jnp.int32, (1, LANES), 1)
        me = lax.axis_index("ao")
        for k, out in zip(shifts, outs):
            first = jnp.minimum((me ^ k) * own // LANES * LANES, columns - width)
            shift = (me ^ k) * own - first
            cut = sum_of(pl.ds(pl.multiple_of(first, LANES), width))
            cut = pltpu.roll(cut, jnp.where(shift == 0, 0, width - shift), 1)
            parcels = [cut[:, j * LANES : (j + 1) * LANES] for j in range(full)]
            if rest:
                groups = LANES // rest
                size = rows // groups
                left = cut[:, full * LANES : (full + 1) * LANES]
                parcel = left[:size]
                for g in range(1, groups):
                    moved = pltpu.roll(left[g * size : (g + 1) * size], g * rest, 1)
                    parcel = jnp.where(lane >= g * rest, moved, parcel)
                parcels.append(parcel)
            out[...] = jnp.concatenate(parcels, axis=0).astype(out.dtype)


def final_kernel(parts, own, *refs):
    out_ref = refs[-1]
    u_own = out_ref.shape[2]
    full, rest = divmod(own, LANES)
    p_from = 0
    for j in range(len(refs) // parts):
        group = refs[j * parts : (j + 1) * parts]
        value = group[0][...]
        for ref in group[1:]:
            value = value + ref[...].astype(jnp.float32)
        rows = value.shape[0] * LANES // own
        pieces = [value[i * rows : (i + 1) * rows] for i in range(full)]
        if rest:
            left = value[full * rows :]
            turns = [left] + [
                pltpu.roll(left, LANES - g * rest, 1) for g in range(1, LANES // rest)
            ]
            pieces.append(jnp.concatenate(turns, axis=0))
        value = jnp.concatenate(pieces, axis=1)[:, :own]
        part = rows // (2 * u_own)
        out_ref[:, p_from : p_from + part] = value.reshape(2, part, u_own, own)
        p_from += part


def swap(size, bit):
    return [(i, i ^ bit) for i in range(size)]


def local(integrals, bra_rows, ket_rows, block_count, pair_count):
    columns = integrals.shape[3]
    general, active = bra_rows.shape[3], ket_rows.shape[3]
    ao_size = lax.axis_size("ao")
    gen_size = lax.axis_size("gen")
    act_size = lax.axis_size("act")
    bra = jnp.swapaxes(bra_rows, 2, 3)
    ket = jnp.swapaxes(ket_rows, 2, 3)
    p_own, u_own = general // gen_size, active // act_size
    dims = (general, active, gen_size, act_size)
    blocks, _, width, _ = integrals.shape
    assert width <= 256
    live = jnp.where(jnp.arange(blocks, dtype=jnp.int32) < block_count, pair_count, 0)
    tail = jnp.broadcast_to(live.astype(bra.dtype)[:, None, None, None], (blocks, 2, 8, width))
    operands = (jnp.concatenate([bra, ket, tail], axis=2), integrals)
    own, width = window_of(columns, ao_size)
    outs = []
    assert (gen_size, act_size) == (4, 2)
    sizes = [2 * part * u_own for part in parts_of(p_own)]
    low = [jax.ShapeDtypeStruct((size, columns), jnp.bfloat16) for size in sizes]

    def move(value, axis, bit):
        return lax.ppermute(value, axis, swap(lax.axis_size(axis), bit))

    def cross(value, odd_first):
        def partner(g, k):
            return (g ^ 2, k) if g % 2 == odd_first else (g, k ^ 1)

        pairs = []
        for g in range(gen_size):
            for k in range(act_size):
                to_g, to_k = partner(g, k)
                pairs.append((g * act_size + k, to_g * act_size + to_k))
        return lax.ppermute(value, ("gen", "act"), pairs)

    kept, got = {}, {}
    for wave, stages in enumerate(STAGES):
        made = list(products(dims, wave, operands))
        for name, _, _ in stages:
            got[name] = move(made.pop(0), "gen", 1)
        for name, _, _ in stages:
            kept[name] = [made.pop(0) for _ in sizes]
        if wave == 0:
            operands = tuple(made)
            whole = jax.ShapeDtypeStruct((sum(sizes), columns), jnp.bfloat16)
            value = small(far_kernel, whole, *kept["far"], got["far"])
            from_far = cross(value, 1)
    parts = ao_size if ao_size <= 4 else 0
    outs = []
    row = 0
    for j, size in enumerate(sizes):
        value = small(
            functools.partial(near_kernel, row), low[j],
            kept["near"][j], got["near"],
        )
        from_near = cross(value, 1)
        value = small(
            functools.partial(two_kernel, row), low[j],
            kept["two"][j], got["two"], from_far,
        )
        from_two = cross(value, 0)
        totals = [
            jax.ShapeDtypeStruct((dense_rows(own, size), LANES), jnp.bfloat16 if k else jnp.float32)
            for k in range(parts)
        ]
        pieces = [None] * max(parts, 1)
        for label, shifts in (("lead", [parts - 1]), ("rest", list(range(parts - 1)))):
            if not parts and label == "rest":
                continue
            made = total_call(
                functools.partial(total_kernel, row, parts, shifts),
                [totals[k] for k in shifts] if parts else [],
                (size, columns), kept["own"][j], got["own"], from_near, from_two,
            )
            for k, piece in zip(shifts if parts else [0], made):
                pieces[k] = piece
        row += size
        if parts:
            outs.append(pieces[0])
            outs += [move(pieces[k], "ao", k) for k in range(1, parts)]
        else:
            total = pieces[0].reshape(size, ao_size, own)
            total = jnp.swapaxes(total, 0, 1).reshape(ao_size * size, own)
            value = lax.psum_scatter(total, "ao", scatter_dimension=0, tiled=True)
            outs.append(value.reshape(2, -1, u_own, own))
    if parts:
        result = jax.ShapeDtypeStruct((2, p_own, u_own, own), jnp.float32)
        return small(functools.partial(final_kernel, parts, own), result, *outs)
    return jnp.concatenate(outs, axis=1)


def solution(mesh):
    spec = P(("ao", "gen", "act"), None, None, None)
    count = P(("ao", "gen", "act"))

    def program(integrals, bra_rows, ket_rows, block_count, pair_count):
        mapped = jax.shard_map(
            local,
            mesh=mesh,
            in_specs=(spec, spec, spec, count, count),
            out_specs=P(None, "gen", "act", "ao"),
            check_vma=False,
        )
        return mapped(integrals, bra_rows, ket_rows, block_count, pair_count)

    return program
```
